256 devices in a mesh: ens: 8 (over x, core), lat: 32 (over z, y).
Axes of the slice: x: 4, y: 4, z: 8, core: 2. Of those that a mesh axis runs over, the one named last changes fastest.
Arguments:
- fields: bfloat16 [16, 24, 192, 1440], P('ens', None, 'lat'), may hold values from -6 to 6
- depth_kernel: float32 [24, 7, 7], replicated, may hold values from -0.875 to 0.875
- mix_weight: bfloat16 [24, 24], replicated, may hold values from -1.25 to 1.25
- legendre: bfloat16 [192, 160, 160], P('lat'), may hold values from -0.875 to 0.875
- truth: bfloat16 [24, 2, 160, 160], replicated, may hold values from -6 to 6
- degree_order: int32 [160], replicated, may hold values from 0 to 159, each once
Outputs:
- grad_fields: bfloat16 [16, 24, 192, 1440], P('ens', None, 'lat')
- score_grad: float32 [16, 24, 2, 160, 160], P('ens', None, None, None, 'lat')
The draws below stay inside these ranges and needn't reach their ends.
Inputs may be any that keep to these rules, and one draw needn't show every extreme that they name: `degree_order`: each degree appears once.
All inputs are finite; a program needn't handle non-finite values.
Results may differ from the reference program's by a relative error of at most 0.02.
Values may be sent and summed in bfloat16 or wider, within the bound.
A program may use at most 128 MiB of HBM per device.

```python
import math
import jax
import jax.numpy as jnp
from jax import lax

C = 24
NLON = 1440
M = 160
L = 160
NLAT = 192
MEMBERS = 16


def strengthened(result, own_key, source, target, shards_of, factor):
    def block_of(dim):
        return (jnp.arange(result.shape[dim]) // (result.shape[dim] // shards_of)).reshape((-1,) + (1,) * (result.ndim - 1 - dim))

    first = jax.random.permutation(own_key, shards_of)[block_of(target)]
    other_side = (block_of(target) + shards_of // 2) % shards_of
    return jnp.where((block_of(source) == first) | (block_of(source) == other_side), factor * result, result)


def level_of(key, extent, pieces, smallest, top_value):
    def one(axis_at, shards_of):
        draws = jax.random.uniform(jax.random.fold_in(jax.random.fold_in(key, 6), axis_at), (shards_of,), jnp.float32, smallest / len(pieces), top_value / len(pieces))
        return jnp.repeat(jnp.exp(draws), extent[axis_at] // shards_of).reshape((-1,) + (1,) * (len(extent) - axis_at - 1))

    loudness = one(*pieces[0])
    for cut in pieces[1:]:
        loudness = loudness * one(*cut)
    return loudness


def gaussian(rng, shape, spread, most, cuts=(), kind=jnp.bfloat16):
    result = jax.random.normal(rng, shape, jnp.float32) * spread
    if len(cuts) > 0:
        result = level_of(rng, shape, cuts, -0.22, 0.18) * result
    return jnp.clip(result, min=-most, max=most).astype(kind)


def heavy_noise(stream_key, dims, deviation, limit, shards, heavy, held_as=jnp.bfloat16):
    drawn = deviation * jax.random.normal(stream_key, dims, jnp.float32)
    if shards:
        drawn = drawn * level_of(stream_key, dims, shards, -0.22, 0.18)
    return jnp.clip(strengthened(drawn, jax.random.fold_in(stream_key, 3), *heavy), -limit, limit).astype(held_as)


def setup_inputs(seed: int = 0) -> dict:
    splits = jax.random.split(jax.random.key(seed), 7)
    return {
        "fields": gaussian(splits[0], (MEMBERS, C, NLAT, NLON), 1.0, 6.0, ((0, 8), (2, 32))),
        "depth_kernel": gaussian(splits[1], (C, 7, 7), 49 ** -0.5, 0.875, (), jnp.float32),
        "mix_weight": gaussian(splits[2], (C, C), C ** -0.5, 1.25),
        "legendre": heavy_noise(splits[3], (NLAT, M, L), NLAT ** -0.5, 0.875, ((0, 32),), (0, 2, 32, 2.75)),
        "truth": gaussian(splits[4], (C, 2, M, L), 1.0, 6.0),
        "degree_order": jax.random.permutation(splits[5], L).astype(jnp.int32),
    }


smooth_width = 0.5

def wave_table():
    columns = jnp.arange(NLON, dtype=jnp.int32)
    orders = jnp.arange(M, dtype=jnp.int32)
    angles = (columns[:, None] * orders[None, :] % NLON).astype(jnp.float32) * (2.0 * math.pi / NLON)
    return (jnp.concatenate([jnp.cos(angles), -jnp.sin(angles)], axis=1) / math.sqrt(NLON)).astype(jnp.bfloat16)

def depthwise(padded, kernel):
    height = padded.shape[-2] - 6
    breadth = padded.shape[-1]
    widened = jnp.concatenate([padded[..., -3:], padded, padded[..., :3]], axis=-1)
    running = jnp.zeros(padded.shape[:-2] + (height, breadth), jnp.float32)
    for row_off in range(7):
        for col_off in range(7):
            running = running + kernel[:, row_off, col_off][:, None, None] * widened[..., row_off:row_off + height, col_off:col_off + breadth]
    return running

def soft_sign(gaps):
    return gaps / jnp.sqrt(gaps * gaps + smooth_width * smooth_width)

def hidden_of(member, kernel):
    padded = jnp.pad(member.astype(jnp.float32), ((0, 0), (3, 3), (0, 0)))
    return padded[:, 3:-3] + depthwise(padded, kernel)

def reference(fields, depth_kernel, mix_weight, legendre, truth, degree_order):
    table = wave_table()
    table_full = legendre.astype(jnp.float32)
    mixing = mix_weight.astype(jnp.float32)

    def forward(member):
        hidden = hidden_of(member, depth_kernel)
        activation = jax.nn.gelu(hidden).astype(jnp.bfloat16)
        mixed_out = jnp.einsum('oc,cij->oij', mixing, activation.astype(jnp.float32)).astype(jnp.bfloat16)
        spectral = jnp.dot(mixed_out, table, preferred_element_type=jnp.float32).astype(jnp.bfloat16)
        spectral = spectral.reshape(C, NLAT, 2, M).astype(jnp.float32)
        return jnp.einsum('cirm,iml->crml', spectral, table_full)
    coeff = lax.map(forward, fields)
    target = truth.astype(jnp.float32)
    ens_count = MEMBERS

    def member_grad(own_coeff):
        pair_sum = lax.optimization_barrier(jnp.sum(soft_sign(own_coeff[None] - coeff), axis=0))
        return soft_sign(own_coeff - target) / ens_count - pair_sum / (ens_count * (ens_count - 1))
    gradient = lax.map(member_grad, coeff)
    score_grad = jnp.take(gradient, degree_order, axis=4)
    sent = gradient.astype(jnp.bfloat16)
    flipped = depth_kernel[:, ::-1, ::-1]

    def backward(inputs):
        member, coeff_grad = inputs
        hidden = hidden_of(member, depth_kernel)
        spec_grad = jnp.einsum('crml,iml->cirm', coeff_grad.astype(jnp.float32), table_full).astype(jnp.bfloat16)
        spec_grad = spec_grad.reshape(C, NLAT, 2 * M)
        mix_grad = jnp.dot(spec_grad, table.T, preferred_element_type=jnp.float32).astype(jnp.bfloat16)
        act_grad = jnp.einsum('oc,oij->cij', mixing, mix_grad.astype(jnp.float32))
        hid_grad = jax.vjp(jax.nn.gelu, hidden)[1](act_grad)[0]
        padded_grad = jnp.pad(hid_grad, ((0, 0), (3, 3), (0, 0)))
        return (hid_grad + depthwise(padded_grad, flipped)).astype(jnp.bfloat16)
    grad_fields = lax.map(backward, (fields, sent))
    return (grad_fields, score_grad)
```

```python
import math

import jax
import jax.numpy as jnp
from jax import lax
from jax.sharding import PartitionSpec as P

NLON = 1440
M = 160
L = 160


smooth_width = 0.5


def padded_2(block, axis, dim, width):
    count = lax.axis_size(axis)
    forward = [(i, i + 1) for i in range(count - 1)]
    backward = [(target, source) for source, target in forward]
    low = lax.ppermute(
        lax.slice_in_dim(block, block.shape[dim] - width, None, axis=dim), axis, forward
    )
    high = lax.ppermute(lax.slice_in_dim(block, 0, width, axis=dim), axis, backward)
    return jnp.concatenate([low, block, high], axis=dim)


def wave_table():
    columns = jnp.arange(NLON, dtype=jnp.int32)
    orders = jnp.arange(M, dtype=jnp.int32)
    angles = (columns[:, None] * orders[None, :] % NLON).astype(jnp.float32) * (
        2.0 * math.pi / NLON
    )
    return (jnp.concatenate([jnp.cos(angles), -jnp.sin(angles)], axis=1) / math.sqrt(NLON)).astype(
        jnp.bfloat16
    )


def depthwise(padded, kernel):
    height = padded.shape[-2] - 6
    breadth = padded.shape[-1]
    widened = jnp.concatenate([padded[..., -3:], padded, padded[..., :3]], axis=-1)
    running = jnp.zeros(padded.shape[:-2] + (height, breadth), jnp.float32)
    for row_off in range(7):
        for col_off in range(7):
            running = (
                running
                + kernel[:, row_off, col_off][:, None, None]
                * widened[..., row_off : row_off + height, col_off : col_off + breadth]
            )
    return running


def soft_sign(gaps):
    return gaps / jnp.sqrt(gaps * gaps + smooth_width * smooth_width)


def local(fields, depth_kernel, mix_weight, legendre, truth, degree_order):
    table = wave_table()
    bands = lax.axis_size("lat")
    orders = M // bands
    mine = lax.all_to_all(legendre, "lat", split_axis=1, concat_axis=0, tiled=True)
    padded = padded_2(fields, "lat", 2, 3).astype(jnp.float32)
    hidden = padded[:, :, 3:-3] + depthwise(padded, depth_kernel)
    activation = jax.nn.gelu(hidden).astype(jnp.bfloat16)
    mixed_out = jnp.einsum(
        "oc,bcij->boij", mix_weight, activation, preferred_element_type=jnp.float32
    ).astype(jnp.bfloat16)
    spectral = jnp.dot(mixed_out, table, preferred_element_type=jnp.float32).astype(jnp.bfloat16)
    spectral = spectral.reshape(spectral.shape[:3] + (2, M))
    spectral = lax.all_to_all(spectral, "lat", split_axis=4, concat_axis=2, tiled=True)
    coeff = jnp.einsum("bcirm,iml->bcrml", spectral, mine, preferred_element_type=jnp.float32)
    share = coeff.shape[1] // lax.axis_size("ens")
    pooled = lax.all_to_all(
        coeff.astype(jnp.bfloat16), "ens", split_axis=1, concat_axis=0, tiled=True
    ).astype(jnp.float32)
    target = lax.dynamic_slice(
        truth,
        (lax.axis_index("ens") * share, 0, lax.axis_index("lat") * orders, 0),
        (share, 2, orders, L),
    ).astype(jnp.float32)
    count = pooled.shape[0]
    pair_sum = jnp.sum(soft_sign(pooled[:, None] - pooled[None]), axis=1)
    pooled_grad = soft_sign(pooled - target[None]) / count - pair_sum / (count * (count - 1))
    sent = lax.all_to_all(
        pooled_grad.astype(jnp.bfloat16), "ens", split_axis=0, concat_axis=1, tiled=True
    )
    spec_grad = jnp.einsum(
        "bcrml,iml->bcirm", sent, mine, preferred_element_type=jnp.float32
    ).astype(jnp.bfloat16)
    spec_grad = lax.all_to_all(spec_grad, "lat", split_axis=2, concat_axis=4, tiled=True)
    chosen = (jnp.arange(L, dtype=jnp.int32)[:, None] == degree_order[None, :]).astype(jnp.bfloat16)
    owned = jnp.einsum("bcrml,lj->bcrmj", sent, chosen, preferred_element_type=jnp.float32).astype(
        jnp.bfloat16
    )
    gradient = lax.all_to_all(owned, "lat", split_axis=4, concat_axis=3, tiled=True).astype(
        jnp.float32
    )
    spec_grad = spec_grad.reshape(spec_grad.shape[:3] + (2 * M,))
    mix_grad = jnp.dot(spec_grad, table.T, preferred_element_type=jnp.float32).astype(jnp.bfloat16)
    act_grad = jnp.einsum("oc,boij->bcij", mix_weight, mix_grad, preferred_element_type=jnp.float32)
    hid_grad = jax.vjp(jax.nn.gelu, hidden)[1](act_grad)[0]
    padded_grad = padded_2(hid_grad.astype(jnp.bfloat16), "lat", 2, 3).astype(hid_grad.dtype)
    grad_fields = (hid_grad + depthwise(padded_grad, depth_kernel[:, ::-1, ::-1])).astype(
        jnp.bfloat16
    )
    return (grad_fields, gradient)


def solution(mesh):
    placed = (P("ens", None, "lat", None), P(), P(), P("lat", None, None), P(), P())
    return jax.shard_map(
        local,
        mesh=mesh,
        in_specs=placed,
        out_specs=(P("ens", None, "lat", None), P("ens", None, None, None, "lat")),
        check_vma=False,
    )
```

```python
import math

import jax
import jax.numpy as jnp
import ml_dtypes
import numpy as np
from jax import lax
from jax.experimental import pallas as pl
from jax.experimental.pallas import tpu as pltpu
from jax.sharding import PartitionSpec as P

C = 24
NLON = 1440
M = 160
L = 160
BANDS = 32
ROWS = 6
ORDERS = M // BANDS
ENS = 8
PART = 112
BF = jnp.bfloat16
F32 = jnp.float32


def wave_table():
    m = (np.arange(BANDS)[None, :] * ORDERS + np.arange(ORDERS)[:, None]).reshape(-1)
    angles = (m[:, None] * np.arange(NLON)[None, :] % NLON) * (2.0 * math.pi / NLON)
    both = np.concatenate([np.cos(angles), -np.sin(angles)], axis=0) / math.sqrt(NLON)
    return both.astype(np.float32).astype(ml_dtypes.bfloat16)


def banded(kernel):
    cols = jnp.broadcast_to(
        jnp.transpose(kernel, (2, 0, 1))[:, None], (7, 3, C, 7)
    ).reshape(504, 7).astype(BF)
    out_row = lax.broadcasted_iota(jnp.int32, (504, 216), 0)
    in_row = lax.broadcasted_iota(jnp.int32, (504, 216), 1)
    same = (out_row % C) == (in_row % C)
    gap = in_row // C - (out_row // C) % 3
    total = jnp.zeros((504, 216), BF)
    for p in range(7):
        total = jnp.where(same & (gap == p), cols[:, p : p + 1], total)
    return total


def wrapped(x):
    return jnp.concatenate([x[:, NLON - 3 :], x, x[:, :93]], axis=1)


def conv_half(low, own, high, weights, ext, prod, k, h):
    if h == 0:
        ext[0:72, :] = wrapped(low[k])
        ext[72:216, :] = wrapped(own[k])
    else:
        ext[0:144, :] = wrapped(own[k])
        ext[144:216, :] = wrapped(high[k])
    prod[...] = jnp.dot(weights[...], ext[...], preferred_element_type=F32)
    total = prod[0:72, 0:NLON]
    for q in range(1, 7):
        total = total + prod[q * 72 : (q + 1) * 72, q : q + NLON]
    return total


def forward_kernel(low, own, high, weights, table, placing, slope, send, ext, prod, act, rows):
    c0 = math.sqrt(2.0 / math.pi)
    for k in range(2):
        for h in range(2):
            part = slice(h * 72, (h + 1) * 72)
            x = own[k, part, :].astype(F32) + conv_half(low, own, high, weights, ext, prod, k, h)
            sq = x * x
            t = jnp.tanh(c0 * x * (1.0 + 0.044715 * sq))
            half = 0.5 * (1.0 + t)
            act[k, part, :] = (x * half).astype(BF)
            slope[k, part, :] = (
                half + 0.5 * x * (1.0 - t * t) * (c0 * (1.0 + 0.134145 * sq))
            ).astype(BF)
    spec = jnp.zeros((2 * M, 384), F32)
    for k in range(2):
        waves = lax.dot_general(
            table[...], act[k], (((1,), (1,)), ((), ())), preferred_element_type=F32
        ).astype(BF)
        spec = spec + jnp.dot(waves, placing[k], preferred_element_type=F32)
    rows[:, 30:32, :] = jnp.zeros((BANDS, 2, 128), F32)
    for a in range(10):
        for t in range(3):
            rows[:, t * 10 + a, :] = spec[a * 32 : (a + 1) * 32, t * 128 : (t + 1) * 128]
    send[...] = rows[...].astype(BF)


def legendre_kernel(recv, leg, coeff, rows):
    rows[...] = recv[...].astype(F32)
    lane = lax.broadcasted_iota(jnp.int32, (L, 128), 1)
    for ml in range(ORDERS):
        acc = []
        for r in range(2):
            a = jnp.concatenate(
                [rows[:, t * 10 + r * 5 + ml, :] for t in range(3)], axis=0
            ).astype(BF)
            for par in range(2):
                acc.append(
                    lax.dot_general(
                        leg[ml, par * 96 : (par + 1) * 96, :],
                        a,
                        (((0,), (0,)), ((), ())),
                        preferred_element_type=F32,
                    )
                )
        first = acc[0] + pltpu.roll(acc[1], 64, 1)
        second = pltpu.roll(acc[2], 64, 1) + acc[3]
        coeff[ml * L : (ml + 1) * L, :] = jnp.where(lane < 64, first, second).astype(BF)
    coeff[800:896, :] = jnp.zeros((96, 128), BF)


def soft_sign(gaps):
    return gaps * lax.rsqrt(gaps * gaps + 0.25)


def score_kernel(pooled, target, grad):
    lane = lax.broadcasted_iota(jnp.int32, (16, 128), 1) % 64

    def step(s, carry):
        at = pl.ds(pl.multiple_of(s * 16, 16), 16)
        x = [pooled[a, at, :].astype(F32) for a in range(ENS)]
        y = [
            jnp.where(lane < 24, pltpu.roll(v, 104, 1), pltpu.roll(v, 24, 1)) for v in x
        ]
        y = [jnp.where(lane < 48, v, 0.0) for v in y]
        goal = target[at, :].astype(F32)
        for a in range(ENS):
            pair = jnp.zeros((16, 128), F32)
            for b in range(ENS):
                if b != a:
                    pair = pair + soft_sign(x[a] - x[b])
                pair = pair + soft_sign(x[a] - y[b])
            grad[a, at, :] = (soft_sign(x[a] - goal) / 16.0 - pair / 240.0).astype(BF)
        return carry

    lax.fori_loop(0, PART // 16, step, 0)


def spread_kernel(grad, leg, chosen, send, owned, rows, more):
    rows[:, 30:32, :] = jnp.zeros((BANDS, 2, 128), F32)
    more[:, 25:32, :] = jnp.zeros((BANDS, 7, 128), F32)
    for ml in range(ORDERS):
        g = grad[ml * L : (ml + 1) * L, :]
        s = jnp.dot(leg[ml], g, preferred_element_type=F32)
        for j in range(ROWS):
            rows[:, ml * 6 + j, :] = s[j * 32 : (j + 1) * 32, :]
        o = jnp.dot(chosen[...], g, preferred_element_type=F32)
        for j in range(5):
            more[:, ml * 5 + j, :] = o[j * 32 : (j + 1) * 32, :]
    send[...] = rows[...].astype(BF)
    owned[...] = more[...].astype(BF)


def backward_kernel(recv, mixing, table, slope, hid, rows, left):
    rows[...] = jnp.dot(
        recv[...].reshape(BANDS * 32, 128), mixing[...], preferred_element_type=F32
    ).reshape(BANDS, 32, 128)
    for i in range(ROWS):
        j = (i % 2) * 3 + i // 2
        q = jnp.concatenate([rows[:, ml * 6 + j, :] for ml in range(ORDERS)], axis=0)
        qt = q.T
        for r in range(2):
            for k in range(2):
                left[r, k, i * 24 : (i + 1) * 24, :] = qt[r * 64 + k * 24 : r * 64 + k * 24 + 24, :]
    for k in range(2):
        grad = jnp.dot(left[0, k].astype(BF), table[0:M, :], preferred_element_type=F32)
        grad = grad + jnp.dot(left[1, k].astype(BF), table[M:, :], preferred_element_type=F32)
        hid[k] = (grad * slope[k].astype(F32)).astype(BF)


def final_kernel(low, own, high, weights, out, ext, prod):
    for k in range(2):
        for h in range(2):
            part = slice(h * 72, (h + 1) * 72)
            out[k, part, :] = (
                own[k, part, :].astype(F32)
                + conv_half(low, own, high, weights, ext, prod, k, h)
            ).astype(BF)


def call(kernel, outs, scratch, *args):
    spec = pl.BlockSpec(memory_space=pltpu.VMEM)
    return pl.pallas_call(
        kernel,
        out_shape=[jax.ShapeDtypeStruct(s, BF) for s in outs],
        in_specs=[spec] * len(args),
        out_specs=[spec] * len(outs),
        scratch_shapes=[pltpu.VMEM(s, d) for s, d in scratch],
        compiler_params=pltpu.CompilerParams(vmem_limit_bytes=48 << 20),
    )(*args)


def edges(x):
    count = lax.axis_size("lat")
    up = [(i, i + 1) for i in range(count - 1)]
    low = lax.ppermute(x[:, 72:], "lat", up)
    high = lax.ppermute(x[:, :72], "lat", [(b, a) for a, b in up])
    return low, high


def swap(x, axis):
    return lax.all_to_all(x, axis, split_axis=0, concat_axis=0, tiled=True)


CONV = [((216, 1536), BF), ((504, 1536), F32)]
CHUNK = (BANDS, 32, 128)


def local(fields, depth_kernel, mix_weight, legendre, truth, degree_order):
    table = jnp.asarray(wave_table())
    x = jnp.transpose(fields, (0, 2, 1, 3)).reshape(2, 144, NLON)
    low, high = edges(x)
    leg = legendre.reshape(3, 2, BANDS, ORDERS, L).transpose(2, 3, 1, 0, 4)
    leg = swap(leg, "lat").transpose(1, 2, 3, 0, 4).reshape(ORDERS, 192, L)
    block = jnp.transpose(mix_weight)
    placing = jnp.stack(
        [
            jnp.kron(jnp.eye(ROWS, dtype=BF), jnp.pad(block, ((0, 0), (24 * k, 40 - 24 * k))))
            for k in range(2)
        ]
    )
    mixing = jnp.kron(
        jnp.eye(2, dtype=BF),
        jnp.pad(jnp.kron(jnp.eye(2, dtype=BF), mix_weight), ((0, 16), (0, 16))),
    )
    weights = banded(depth_kernel)
    flipped = banded(depth_kernel[:, ::-1, ::-1])
    lanes = np.arange(128)
    spot = (
        (lanes[None, None, :] // 64 == np.arange(2)[None, :, None])
        & (lanes[None, None, :] % 64 < 48)
        & (lanes[None, None, :] % 64 % 24 == np.arange(C)[:, None, None])
    )
    mine = lax.dynamic_slice_in_dim(truth, lax.axis_index("lat") * ORDERS, ORDERS, 2)
    target = jnp.einsum(
        "crml,crn->mln", mine, jnp.asarray(spot, BF), preferred_element_type=F32
    ).astype(BF)
    target = jnp.pad(target.reshape(800, 128), ((0, 96), (0, 0)))
    target = lax.dynamic_slice_in_dim(target, lax.axis_index("ens") * PART, PART, 0)
    place = degree_order.reshape(BANDS, 5).T.reshape(L)
    chosen = (place[:, None] == jnp.arange(L, dtype=jnp.int32)[None, :]).astype(BF)

    slope, send = call(
        forward_kernel,
        [(2, 144, NLON), CHUNK],
        CONV + [((2, 144, NLON), BF), (CHUNK, F32)],
        low, x, high, weights, table, placing,
    )
    (coeff,) = call(legendre_kernel, [(896, 128)], [(CHUNK, F32)], swap(send, "lat"), leg)
    pooled = swap(coeff.reshape(ENS, PART, 128), "ens")
    (grad,) = call(score_kernel, [(ENS, PART, 128)], [], pooled, target)
    grad = swap(grad, "ens").reshape(896, 128)
    send, owned = call(
        spread_kernel, [CHUNK, CHUNK], [(CHUNK, F32), (CHUNK, F32)], grad, leg, chosen
    )
    recv = swap(send, "lat")
    owned = swap(owned, "lat")
    (hid,) = call(
        backward_kernel,
        [(2, 144, NLON)],
        [(CHUNK, F32), ((2, 2, 144, M), F32)],
        recv, mixing, table, slope,
    )
    low, high = edges(hid)
    (out,) = call(final_kernel, [(2, 144, NLON)], CONV, low, hid, high, flipped)
    grad_fields = jnp.transpose(out.reshape(2, ROWS, C, NLON), (0, 2, 1, 3))
    score = owned[:, :25].reshape(BANDS, ORDERS, 5, 2, 64)[..., :48]
    score = score.reshape(BANDS, ORDERS, 5, 2, 2, C).transpose(4, 5, 3, 0, 1, 2)
    return grad_fields, score.reshape(2, C, 2, M, 5).astype(F32)


def solution(mesh):
    placed = (P("ens", None, "lat", None), P(), P(), P("lat", None, None), P(), P())
    return jax.shard_map(
        local,
        mesh=mesh,
        in_specs=placed,
        out_specs=(P("ens", None, "lat", None), P("ens", None, None, None, "lat")),
        check_vma=False,
    )
```

```python
import math

import jax
import jax.numpy as jnp
import ml_dtypes
import numpy as np
from jax import lax
from jax.experimental import pallas as pl
from jax.experimental.pallas import tpu as pltpu
from jax.sharding import PartitionSpec as P

C = 24
NLON = 1440
M = 160
L = 160
BANDS = 32
ROWS = 6
ORDERS = M // BANDS
ENS = 8
PART = 112
BF = jnp.bfloat16
F32 = jnp.float32
MESH = pl.DeviceIdType.MESH


def wave_table():
    m = (np.arange(BANDS)[None, :] * ORDERS + np.arange(ORDERS)[:, None]).reshape(-1)
    angles = (m[:, None] * np.arange(NLON)[None, :] % NLON) * (2.0 * math.pi / NLON)
    both = np.concatenate([np.cos(angles), -np.sin(angles)], axis=0) / math.sqrt(NLON)
    return both.astype(np.float32).astype(ml_dtypes.bfloat16)


def wrapped(x):
    return jnp.concatenate([x[:, NLON - 3 :], x, x[:, :93]], axis=1)


def spread_weights(cols, dst, tmp, flip):
    lane = lax.broadcasted_iota(jnp.int32, (C, 216), 1)
    same = lane % C == lax.broadcasted_iota(jnp.int32, (C, 216), 0)
    for h in range(2):
        row = lane // C
        window = lax.rem(row + 3, 9) if h == 0 else row
        masks = [same & (window == g) for g in range(9)]
        for q in range(7):
            taps = []
            for p in range(7):
                a, b = (6 - q, 6 - p) if flip else (q, p)
                taps.append(jnp.broadcast_to(cols[a, :, b : b + 1], (C, 216)))
            for i in range(3):
                total = jnp.zeros((C, 216), F32)
                for p in range(7):
                    total = jnp.where(masks[i + p], taps[p], total)
                tmp[q * 72 + i * 24 : q * 72 + i * 24 + 24, :] = total
        dst[h] = tmp[...].astype(BF)


def conv_half(weights, ext, prod, h):
    prod[...] = jnp.dot(weights[h], ext[...], preferred_element_type=F32)
    total = prod[0:72, 0:NLON]
    for q in range(1, 7):
        total = total + prod[q * 72 : (q + 1) * 72, q : q + NLON]
    return total


def soft_sign(gaps):
    return gaps * lax.rsqrt(gaps * gaps + 0.25)


class Exchange:
    def __init__(self, axis, count, me, block, slot, sent, landed, sems):
        self.axis, self.count, self.me = axis, count, me
        self.block, self.slot = block, slot
        self.sent, self.landed, self.sems = sent, landed, sems

    def copy(self, source, target, peer):
        return pltpu.make_async_remote_copy(
            src_ref=source,
            dst_ref=target,
            send_sem=self.sems.at[0],
            recv_sem=self.sems.at[1],
            device_id={self.axis: peer},
            device_id_type=MESH,
        )

    def start(self):
        def step(s, carry):
            peer = lax.rem(self.me + s, self.count)
            self.copy(self.block(peer), self.slot(self.me), peer).start()
            return carry

        lax.fori_loop(1, self.count, step, 0)

    def whole(self):
        return self.copy(self.sent, self.landed, lax.rem(self.me + 1, self.count))

    def arrived(self):
        self.whole().wait_recv()

    def done(self):
        self.whole().wait_send()


def kernel(
    x, legl, cols, table, placing, mixing, target, chosen,
    out, score,
    low, high, low2, high2, weights, flipped, wtmp, ext, prod, act, slope, hid,
    legf, legsend, legrecv, leg,
    rows, more, send1, recv1, coeff, pooled, grads, gback, send4, recv4, send5, recv5,
    left, turn,
    halo_sems, halo2_sems, leg_sems, sems1, sems2, sems3, sems4, sems5,
):
    me = lax.axis_index("lat")
    em = lax.axis_index("ens")
    after = lax.rem(me + 1, BANDS)
    before = lax.rem(me + BANDS - 1, BANDS)

    barrier = pltpu.get_barrier_semaphore()

    def greet(axis, count, mine):
        def step(s, carry):
            pl.semaphore_signal(
                barrier, 1, device_id={axis: lax.rem(mine + s, count)}, device_id_type=MESH
            )
            return carry

        lax.fori_loop(1, count, step, 0)

    greet("lat", BANDS, me)
    greet("ens", ENS, em)
    pl.semaphore_wait(barrier, BANDS - 1 + ENS - 1)

    def halo(source, lo, hi, sems, k):
        return (
            pltpu.make_async_remote_copy(
                src_ref=source.at[k, 1], dst_ref=lo.at[k],
                send_sem=sems.at[0, k], recv_sem=sems.at[1, k],
                device_id={"lat": after}, device_id_type=MESH,
            ),
            pltpu.make_async_remote_copy(
                src_ref=source.at[k, 0], dst_ref=hi.at[k],
                send_sem=sems.at[2, k], recv_sem=sems.at[3, k],
                device_id={"lat": before}, device_id_type=MESH,
            ),
        )

    halos = [halo(x, low, high, halo_sems, k) for k in range(2)]
    for pair in halos:
        for copy in pair:
            copy.start()

    for i in range(ROWS):
        j = (i % 2) * 3 + i // 2
        legf[0] = legl[i, :, 0:128].astype(F32)
        legf[1] = jnp.concatenate(
            [legl[i, :, 128:L].astype(F32), jnp.zeros((M, 256 - L), F32)], axis=1
        )
        for ml in range(ORDERS):
            for b in range(2):
                more[b, :, ml * 6 + j, :] = legf[b, pl.ds(ml, BANDS, stride=ORDERS), :]
    for b in range(2):
        more[b, :, 30:32, :] = jnp.zeros((BANDS, 2, 128), F32)
        legsend[:, b] = more[b].astype(BF)
    legx = Exchange(
        "lat", BANDS, me, lambda p: legsend.at[p], lambda m: legrecv.at[m],
        legsend.at[pl.ds(0, BANDS - 1)], legrecv.at[pl.ds(0, BANDS - 1)], leg_sems,
    )
    legx.start()
    legrecv[me] = legsend[me]
    spread_weights(cols, weights, wtmp, False)

    def fill_halo(lo, hi, k, h):
        if h == 0:
            edge = wrapped(lo[k].astype(F32))
            ext[144:216, :] = jnp.where(me > 0, edge, 0.0).astype(BF)
        else:
            edge = wrapped(hi[k].astype(F32))
            ext[144:216, :] = jnp.where(me < BANDS - 1, edge, 0.0).astype(BF)

    c0 = math.sqrt(2.0 / math.pi)
    spec = jnp.zeros((2 * M, 384), F32)
    for k in range(2):
        ext[0:72, :] = wrapped(x[k, 0])
        ext[72:144, :] = wrapped(x[k, 1])
        for h in range(2):
            halos[k][h].wait_recv()
            fill_halo(low, high, k, h)
            v = x[k, h].astype(F32) + conv_half(weights, ext, prod, h)
            sq = v * v
            t = jnp.tanh(c0 * v * (1.0 + 0.044715 * sq))
            half = 0.5 * (1.0 + t)
            act[h * 72 : (h + 1) * 72, :] = (v * half).astype(BF)
            slope[k, h] = (half + 0.5 * v * (1.0 - t * t) * (c0 * (1.0 + 0.134145 * sq))).astype(BF)
        waves = lax.dot_general(
            table[...], act[...], (((1,), (1,)), ((), ())), preferred_element_type=F32
        ).astype(BF)
        spec = spec + jnp.dot(waves, placing[k], preferred_element_type=F32)
    rows[:, 30:32, :] = jnp.zeros((BANDS, 2, 128), F32)
    for a in range(10):
        for t in range(3):
            rows[:, t * 10 + a, :] = spec[a * 32 : (a + 1) * 32, t * 128 : (t + 1) * 128]
    send1[...] = rows[...].astype(BF)
    x1 = Exchange(
        "lat", BANDS, me, lambda p: send1.at[p], lambda m: recv1.at[m],
        send1.at[pl.ds(0, BANDS - 1)], recv1.at[pl.ds(0, BANDS - 1)], sems1,
    )
    x1.start()
    recv1[me] = send1[me]

    legx.arrived()
    for b in range(2):
        more[b] = legrecv[:, b].astype(F32)
    for ml in range(ORDERS):
        for j in range(ROWS):
            at = slice(j * 32, (j + 1) * 32)
            leg[ml, at, 0:128] = more[0, :, ml * 6 + j, :].astype(BF)
            leg[ml, at, 128:L] = more[1, :, ml * 6 + j, 0 : L - 128].astype(BF)

    x1.arrived()
    rows[...] = recv1[...].astype(F32)
    lane = lax.broadcasted_iota(jnp.int32, (L, 128), 1)
    for ml in range(ORDERS):
        acc = []
        for r in range(2):
            a = jnp.concatenate(
                [rows[:, t * 10 + r * 5 + ml, :] for t in range(3)], axis=0
            ).astype(BF)
            for par in range(2):
                acc.append(
                    lax.dot_general(
                        leg[ml, par * 96 : (par + 1) * 96, :],
                        a,
                        (((0,), (0,)), ((), ())),
                        preferred_element_type=F32,
                    )
                )
        first = acc[0] + pltpu.roll(acc[1], 64, 1)
        second = pltpu.roll(acc[2], 64, 1) + acc[3]
        coeff[ml * L : (ml + 1) * L, :] = jnp.where(lane < 64, first, second).astype(BF)
    coeff[800:896, :] = jnp.zeros((96, 128), BF)

    def piece(ref, e):
        return ref.at[pl.ds(pl.multiple_of(e * PART, 16), PART)]

    x2 = Exchange(
        "ens", ENS, em, lambda p: piece(coeff, p), lambda m: pooled.at[m],
        coeff.at[pl.ds(0, (ENS - 1) * PART)], pooled.at[pl.ds(0, ENS - 1)], sems2,
    )
    x2.start()
    pooled[em] = piece(coeff, em)[...]
    spread_weights(cols, flipped, wtmp, True)
    x2.arrived()

    small = lax.broadcasted_iota(jnp.int32, (16, 128), 1) % 64

    def step(s, carry):
        at = pl.ds(pl.multiple_of(s * 16, 16), 16)
        u = [pooled[a, at, :].astype(F32) for a in range(ENS)]
        w = [jnp.where(small < 24, pltpu.roll(v, 104, 1), pltpu.roll(v, 24, 1)) for v in u]
        w = [jnp.where(small < 48, v, 0.0) for v in w]
        goal = target[at, :].astype(F32)
        for a in range(ENS):
            pair = jnp.zeros((16, 128), F32)
            for b in range(ENS):
                if b != a:
                    pair = pair + soft_sign(u[a] - u[b])
                pair = pair + soft_sign(u[a] - w[b])
            grads[a, at, :] = (soft_sign(u[a] - goal) / 16.0 - pair / 240.0).astype(BF)
        return carry

    lax.fori_loop(0, PART // 16, step, 0)
    x3 = Exchange(
        "ens", ENS, em, lambda p: grads.at[p], lambda m: piece(gback, m),
        grads.at[pl.ds(0, ENS - 1)], gback.at[pl.ds(0, (ENS - 1) * PART)], sems3,
    )
    x3.start()
    piece(gback, em)[...] = grads[em]
    x3.arrived()

    for ml in range(ORDERS):
        s = jnp.dot(leg[ml], gback[ml * L : (ml + 1) * L, :], preferred_element_type=F32)
        for j in range(ROWS):
            rows[:, ml * 6 + j, :] = s[j * 32 : (j + 1) * 32, :]
    send4[...] = rows[...].astype(BF)
    x4 = Exchange(
        "lat", BANDS, me, lambda p: send4.at[p], lambda m: recv4.at[m],
        send4.at[pl.ds(0, BANDS - 1)], recv4.at[pl.ds(0, BANDS - 1)], sems4,
    )
    x4.start()
    recv4[me] = send4[me]
    for ml in range(ORDERS):
        o = jnp.dot(chosen[...], gback[ml * L : (ml + 1) * L, :], preferred_element_type=F32)
        for j in range(5):
            rows[:, ml * 5 + j, :] = o[j * 32 : (j + 1) * 32, :]
    send5[...] = rows[...].astype(BF)
    x5 = Exchange(
        "lat", BANDS, me, lambda p: send5.at[p], lambda m: recv5.at[m],
        send5.at[pl.ds(0, BANDS - 1)], recv5.at[pl.ds(0, BANDS - 1)], sems5,
    )
    x5.start()
    recv5[me] = send5[me]

    x4.arrived()
    rows[...] = jnp.dot(
        recv4[...].reshape(BANDS * 32, 128), mixing[...], preferred_element_type=F32
    ).reshape(BANDS, 32, 128)
    for i in range(ROWS):
        j = (i % 2) * 3 + i // 2
        q = jnp.concatenate([rows[:, ml * 6 + j, :] for ml in range(ORDERS)], axis=0)
        qt = q.T
        for r in range(2):
            for k in range(2):
                left[r, k, i * 24 : (i + 1) * 24, :] = qt[r * 64 + k * 24 : r * 64 + k * 24 + 24, :]
    halos2 = []
    for k in range(2):
        grad = jnp.dot(left[0, k].astype(BF), table[0:M, :], preferred_element_type=F32)
        grad = grad + jnp.dot(left[1, k].astype(BF), table[M:, :], preferred_element_type=F32)
        for h in range(2):
            hid[k, h] = (grad[h * 72 : (h + 1) * 72] * slope[k, h].astype(F32)).astype(BF)
        pair = halo(hid, low2, high2, halo2_sems, k)
        for copy in pair:
            copy.start()
        halos2.append(pair)

    x5.arrived()
    rows[...] = recv5[...].astype(F32)
    for j in range(5):
        for ml in range(ORDERS):
            turn[pl.ds(ml, BANDS, stride=ORDERS), :] = rows[:, ml * 5 + j, :]
        qt = turn[...].T
        for r in range(2):
            for k in range(2):
                score[k, :, j, r, :] = qt[r * 64 + k * 24 : r * 64 + k * 24 + 24, :]

    for k in range(2):
        ext[0:72, :] = wrapped(hid[k, 0])
        ext[72:144, :] = wrapped(hid[k, 1])
        for h in range(2):
            halos2[k][h].wait_recv()
            fill_halo(low2, high2, k, h)
            out[k, h] = (hid[k, h].astype(F32) + conv_half(flipped, ext, prod, h)).astype(BF)

    for pairs in (halos, halos2):
        for pair in pairs:
            for copy in pair:
                copy.wait_send()
    for exchange in (legx, x1, x2, x3, x4, x5):
        exchange.done()


HALF = (2, 2, 72, NLON)
CHUNK = (BANDS, 32, 128)


def whole(*args):
    spec = pl.BlockSpec(memory_space=pltpu.VMEM)
    pair = pltpu.SemaphoreType.DMA((2,))
    scratch = [
        ((2, 72, NLON), BF), ((2, 72, NLON), BF), ((2, 72, NLON), BF), ((2, 72, NLON), BF),
        ((2, 504, 216), BF), ((2, 504, 216), BF), ((504, 216), F32),
        ((216, 1536), BF), ((504, 1536), F32), ((144, NLON), BF), (HALF, BF), (HALF, BF),
        ((2, M, 128), F32), ((BANDS, 2, 32, 128), BF), ((BANDS, 2, 32, 128), BF), ((ORDERS, 192, L), BF),
        (CHUNK, F32), ((2,) + CHUNK, F32), (CHUNK, BF), (CHUNK, BF),
        ((896, 128), BF), ((ENS, PART, 128), BF), ((ENS, PART, 128), BF), ((896, 128), BF),
        (CHUNK, BF), (CHUNK, BF), (CHUNK, BF), (CHUNK, BF),
        ((2, 2, 144, M), F32), ((M, 128), F32),
    ]
    return pl.pallas_call(
        kernel,
        out_shape=[
            jax.ShapeDtypeStruct(HALF, BF),
            jax.ShapeDtypeStruct((2, C, 5, 2, M), F32),
        ],
        in_specs=[spec] * len(args),
        out_specs=[spec, spec],
        scratch_shapes=[pltpu.VMEM(s, d) for s, d in scratch]
        + [pltpu.SemaphoreType.DMA((4, 2))] * 2
        + [pair] * 6,
        compiler_params=pltpu.CompilerParams(
            vmem_limit_bytes=52 << 20, collective_id=0, has_side_effects=True
        ),
    )(*args)


def local(fields, depth_kernel, mix_weight, legendre, truth, degree_order):
    table = jnp.asarray(wave_table())
    x = jnp.transpose(fields, (0, 2, 1, 3)).reshape(HALF)
    block = jnp.transpose(mix_weight)
    placing = jnp.stack(
        [
            jnp.kron(jnp.eye(ROWS, dtype=BF), jnp.pad(block, ((0, 0), (24 * k, 40 - 24 * k))))
            for k in range(2)
        ]
    )
    mixing = jnp.kron(
        jnp.eye(2, dtype=BF),
        jnp.pad(jnp.kron(jnp.eye(2, dtype=BF), mix_weight), ((0, 16), (0, 16))),
    )
    lanes = np.arange(128)
    spot = (
        (lanes[None, None, :] // 64 == np.arange(2)[None, :, None])
        & (lanes[None, None, :] % 64 < 48)
        & (lanes[None, None, :] % 64 % 24 == np.arange(C)[:, None, None])
    )
    mine = lax.dynamic_slice_in_dim(truth, lax.axis_index("lat") * ORDERS, ORDERS, 2)
    target = jnp.einsum(
        "crml,crn->mln", mine, jnp.asarray(spot, BF), preferred_element_type=F32
    ).astype(BF)
    target = jnp.pad(target.reshape(800, 128), ((0, 96), (0, 0)))
    target = lax.dynamic_slice_in_dim(target, lax.axis_index("ens") * PART, PART, 0)
    place = degree_order.reshape(BANDS, 5).T.reshape(L)
    chosen = (place[:, None] == jnp.arange(L, dtype=jnp.int32)[None, :]).astype(BF)
    cols = jnp.transpose(depth_kernel, (2, 0, 1))
    out, score = whole(x, legendre, cols, table, placing, mixing, target, chosen)
    grad_fields = jnp.transpose(out.reshape(2, ROWS, C, NLON), (0, 2, 1, 3))
    return grad_fields, jnp.transpose(score, (0, 1, 3, 4, 2))


def solution(mesh):
    placed = (P("ens", None, "lat", None), P(), P(), P("lat", None, None), P(), P())
    return jax.shard_map(
        local,
        mesh=mesh,
        in_specs=placed,
        out_specs=(P("ens", None, "lat", None), P("ens", None, None, None, "lat")),
        check_vma=False,
    )
```

```python
import math

import jax
import jax.numpy as jnp
import ml_dtypes
import numpy as np
from jax import lax
from jax.experimental import pallas as pl
from jax.experimental.pallas import tpu as pltpu
from jax.sharding import PartitionSpec as P

C = 24
NLON = 1440
M = 160
L = 160
BANDS = 32
ROWS = 6
ORDERS = M // BANDS
ENS = 8
PART = 112
BF = jnp.bfloat16
F32 = jnp.float32
MESH = pl.DeviceIdType.MESH


def wave_table():
    m = (np.arange(BANDS)[None, :] * ORDERS + np.arange(ORDERS)[:, None]).reshape(-1)
    angles = (m[:, None] * np.arange(NLON)[None, :] % NLON) * (2.0 * math.pi / NLON)
    both = np.concatenate([np.cos(angles), -np.sin(angles)], axis=0) / math.sqrt(NLON)
    return both.astype(np.float32).astype(ml_dtypes.bfloat16)


def wrapped(x):
    return jnp.concatenate([x[:, NLON - 3 :], x, x[:, :93]], axis=1)


def iota(shape, axis):
    return lax.broadcasted_iota(jnp.int32, shape, axis)


def onehot(hit):
    return jnp.where(hit, 1.0, 0.0).astype(BF)


def tile_taps(kern, taps):
    again = onehot(iota((C, 216), 1) % C == iota((C, 216), 0))
    for p in range(7):
        taps[p] = jnp.dot(kern[p].astype(BF), again, preferred_element_type=F32)


def spread_weights(taps, dst, tmp, flip):
    lane = iota((C, 216), 1)
    same = lane % C == iota((C, 216), 0)
    for h in range(2):
        row = lane // C
        window = lax.rem(row + 3, 9) if h == 0 else row
        masks = [same & (window == g) for g in range(9)]
        for q in range(7):
            tap = []
            for p in range(7):
                a, b = (6 - p, 6 - q) if flip else (p, q)
                tap.append(jnp.broadcast_to(taps[a, b : b + 1, :], (C, 216)))
            for i in range(3):
                total = jnp.zeros((C, 216), F32)
                for p in range(7):
                    total = jnp.where(masks[i + p], tap[p], total)
                tmp[q * 72 + i * 24 : q * 72 + i * 24 + 24, :] = total
        dst[h] = tmp[...].astype(BF)


def place_mix(mix, placing):
    row = iota((144, C), 0)
    tall = lax.dot_general(
        onehot(row % C == iota((144, C), 1)), mix[...], (((1,), (1,)), ((), ())),
        preferred_element_type=F32,
    ).astype(BF)
    for k in range(2):
        wide = onehot(iota((C, 384), 1) % 64 == iota((C, 384), 0) + C * k)
        full = jnp.dot(tall, wide, preferred_element_type=F32)
        same = iota((144, 384), 0) // C == iota((144, 384), 1) // 64
        placing[k] = jnp.where(same, full, 0.0).astype(BF)


def group(v):
    return v // 64 * 2 + v % 64 // C, v % 64 % C


def mix_lanes(mix):
    rk, o = group(iota((128, C), 0))
    tall = jnp.dot(onehot(o == iota((128, C), 1)), mix[...], preferred_element_type=F32).astype(BF)
    rk, c = group(iota((C, 128), 1))
    full = jnp.dot(tall, onehot(c == iota((C, 128), 0)), preferred_element_type=F32)
    a, b = iota((128, 128), 0), iota((128, 128), 1)
    same = (group(a)[0] == group(b)[0]) & (a % 64 < 48) & (b % 64 < 48)
    return jnp.where(same, full, 0.0).astype(BF)


def conv_half(weights, ext, prod, h):
    prod[...] = jnp.dot(weights[h], ext[...], preferred_element_type=F32)
    total = prod[0:72, 0:NLON]
    for q in range(1, 7):
        total = total + prod[q * 72 : (q + 1) * 72, q : q + NLON]
    return total


def soft_sign(gaps):
    return gaps * lax.rsqrt(gaps * gaps + 0.25)


class Exchange:
    def __init__(self, axis, count, me, block, slot, sent, landed, sems):
        self.axis, self.count, self.me = axis, count, me
        self.block, self.slot = block, slot
        self.sent, self.landed, self.sems = sent, landed, sems

    def copy(self, source, target, peer):
        return pltpu.make_async_remote_copy(
            src_ref=source,
            dst_ref=target,
            send_sem=self.sems.at[0],
            recv_sem=self.sems.at[1],
            device_id={self.axis: peer},
            device_id_type=MESH,
        )

    def start(self):
        def step(s, carry):
            peer = lax.rem(self.me + s, self.count)
            self.copy(self.block(peer), self.slot(self.me), peer).start()
            return carry

        lax.fori_loop(1, self.count, step, 0)

    def whole(self):
        return self.copy(self.sent, self.landed, lax.rem(self.me + 1, self.count))

    def arrived(self):
        self.whole().wait_recv()

    def done(self):
        self.whole().wait_send()


def kernel(
    x_hbm, leg_hbm, kern, table_hbm, mix, truth, order,
    out, score,
    x, legl, table, window, wide, taps, placing, target, chosen,
    low, high, low2, high2, weights, flipped, wtmp, ext, prod, act, slope, hid,
    legf, legsend, legrecv, legall, leg,
    rows, stage, more, send1, recv1, coeff, pooled, grads, gback, send4, recv4, send5, recv5,
    left, turn,
    load_sems, halo_sems, halo2_sems, leg_sems, leg2_sems, sems1, sems2, sems3, sems4, sems5,
):
    me = lax.axis_index("lat")
    em = lax.axis_index("ens")
    after = lax.rem(me + 1, BANDS)
    before = lax.rem(me + BANDS - 1, BANDS)

    m0 = me * ORDERS
    base = jnp.minimum(m0 // 8 * 8, M - 16)
    loads = [
        pltpu.make_async_copy(source, target_, load_sems.at[n])
        for n, (source, target_) in enumerate(
            [
                (leg_hbm, legl),
                (x_hbm, x),
                (truth.at[:, :, pl.ds(pl.multiple_of(base, 8), 16), :], window),
                (table_hbm, table),
            ]
        )
    ]
    for load in loads:
        load.start()
    barrier = pltpu.get_barrier_semaphore()

    def greet(axis, count, mine):
        def step(s, carry):
            pl.semaphore_signal(
                barrier, 1, device_id={axis: lax.rem(mine + s, count)}, device_id_type=MESH
            )
            return carry

        lax.fori_loop(1, count, step, 0)

    greet("lat", BANDS, me)
    greet("ens", ENS, em)
    pl.semaphore_wait(barrier, BANDS - 1 + ENS - 1)

    def halo(source, lo, hi, sems, k):
        return (
            pltpu.make_async_remote_copy(
                src_ref=source.at[k, 1], dst_ref=lo.at[k],
                send_sem=sems.at[0, k], recv_sem=sems.at[1, k],
                device_id={"lat": after}, device_id_type=MESH,
            ),
            pltpu.make_async_remote_copy(
                src_ref=source.at[k, 0], dst_ref=hi.at[k],
                send_sem=sems.at[2, k], recv_sem=sems.at[3, k],
                device_id={"lat": before}, device_id_type=MESH,
            ),
        )

    halos = [halo(x_hbm, low, high, halo_sems, k) for k in range(2)]
    for pair in halos:
        for copy in pair:
            copy.start()

    loads[0].wait()
    for i in range(ROWS):
        legf[0, i] = legl[i, :, 0:128].astype(F32)
        legf[1, i] = jnp.concatenate(
            [legl[i, :, 128:L].astype(F32), jnp.zeros((M, 256 - L), F32)], axis=1
        )
    for q in range(4):
        n = jnp.minimum(em * 4 + q, 29)
        for b in range(2):
            stage[:, q * 2 + b, :] = legf[
                b, n // ORDERS, pl.ds(lax.rem(n, ORDERS), BANDS, stride=ORDERS), :
            ]
    legsend[...] = stage[...].astype(BF)
    legx = Exchange(
        "lat", BANDS, me, lambda p: legsend.at[p], lambda m: legrecv.at[m],
        legsend.at[pl.ds(0, BANDS - 1)], legrecv.at[pl.ds(0, BANDS - 1)], leg_sems,
    )
    legx.start()
    legrecv[me] = legsend[me]
    tile_taps(kern, taps)
    spread_weights(taps, weights, wtmp, False)
    place_mix(mix, placing)

    def fill_halo(lo, hi, k, h):
        if h == 0:
            edge = wrapped(lo[k].astype(F32))
            ext[144:216, :] = jnp.where(me > 0, edge, 0.0).astype(BF)
        else:
            edge = wrapped(hi[k].astype(F32))
            ext[144:216, :] = jnp.where(me < BANDS - 1, edge, 0.0).astype(BF)

    loads[1].wait()
    loads[3].wait()
    c0 = math.sqrt(2.0 / math.pi)
    spec = jnp.zeros((2 * M, 384), F32)
    for k in range(2):
        ext[0:72, :] = wrapped(x[k, 0])
        ext[72:144, :] = wrapped(x[k, 1])
        for h in range(2):
            halos[k][h].wait_recv()
            fill_halo(low, high, k, h)
            v = x[k, h].astype(F32) + conv_half(weights, ext, prod, h)
            sq = v * v
            t = jnp.tanh(c0 * v * (1.0 + 0.044715 * sq))
            half = 0.5 * (1.0 + t)
            act[h * 72 : (h + 1) * 72, :] = (v * half).astype(BF)
            slope[k, h] = (half + 0.5 * v * (1.0 - t * t) * (c0 * (1.0 + 0.134145 * sq))).astype(BF)
        waves = lax.dot_general(
            table[...], act[...], (((1,), (1,)), ((), ())), preferred_element_type=F32
        ).astype(BF)
        spec = spec + jnp.dot(waves, placing[k], preferred_element_type=F32)
        if k == 0:
            legx.arrived()
            legx2 = Exchange(
                "ens", ENS, em, lambda p: legrecv, lambda m: legall.at[m],
                legall.at[pl.ds(0, ENS - 1)], legall.at[pl.ds(0, ENS - 1)], leg2_sems,
            )
            legx2.start()
            legall[em] = legrecv[...]
    rows[:, 30:32, :] = jnp.zeros((BANDS, 2, 128), F32)
    for a in range(10):
        for t in range(3):
            rows[:, t * 10 + a, :] = spec[a * 32 : (a + 1) * 32, t * 128 : (t + 1) * 128]
    send1[...] = rows[...].astype(BF)
    x1 = Exchange(
        "lat", BANDS, me, lambda p: send1.at[p], lambda m: recv1.at[m],
        send1.at[pl.ds(0, BANDS - 1)], recv1.at[pl.ds(0, BANDS - 1)], sems1,
    )
    x1.start()
    recv1[me] = send1[me]

    loads[2].wait()
    wide[0] = window[:, :, :, 0:128].astype(F32).reshape(2 * C, 16, 128)
    wide[1] = jnp.concatenate(
        [
            window[:, :, :, 128:L].astype(F32).reshape(2 * C, 16, L - 128),
            jnp.zeros((2 * C, 16, 256 - L), F32),
        ],
        axis=2,
    )
    cr, at = iota((2 * C, 128), 0), iota((2 * C, 128), 1)
    spot = onehot((at // 64 == cr % 2) & (at % 64 < 48) & (at % 64 % C == cr // 2))
    for ml in range(ORDERS):
        for b in range(2):
            part = wide[b, :, m0 - base + ml, :].astype(BF)
            t = lax.dot_general(part, spot, (((0,), (0,)), ((), ())), preferred_element_type=F32)
            if b == 0:
                target[ml * L : ml * L + 128, :] = t.astype(BF)
            else:
                target[ml * L + 128 : ml * L + L, :] = t[0 : L - 128].astype(BF)
    target[800:896, :] = jnp.zeros((96, 128), BF)
    place = iota((L, L), 0)
    spots = onehot(iota((L, L), 1) == place % BANDS * 5 + place // BANDS)
    kept = onehot(place == jnp.broadcast_to(order[...], (L, L)))
    chosen[...] = lax.dot_general(
        spots, kept, (((1,), (1,)), ((), ())), preferred_element_type=F32
    ).astype(BF)

    legx2.arrived()
    more[...] = legall[...].astype(F32)
    for ml in range(ORDERS):
        for i in range(ROWS):
            n, j = i * ORDERS + ml, (i % 2) * 3 + i // 2
            at = slice(j * 32, (j + 1) * 32)
            leg[ml, at, 0:128] = more[n // 4, :, n % 4 * 2, :].astype(BF)
            leg[ml, at, 128:L] = more[n // 4, :, n % 4 * 2 + 1, 0 : L - 128].astype(BF)

    x1.arrived()
    rows[...] = recv1[...].astype(F32)
    lane = lax.broadcasted_iota(jnp.int32, (L, 128), 1)
    for ml in range(ORDERS):
        acc = []
        for r in range(2):
            a = jnp.concatenate(
                [rows[:, t * 10 + r * 5 + ml, :] for t in range(3)], axis=0
            ).astype(BF)
            for par in range(2):
                acc.append(
                    lax.dot_general(
                        leg[ml, par * 96 : (par + 1) * 96, :],
                        a,
                        (((0,), (0,)), ((), ())),
                        preferred_element_type=F32,
                    )
                )
        first = acc[0] + pltpu.roll(acc[1], 64, 1)
        second = pltpu.roll(acc[2], 64, 1) + acc[3]
        coeff[ml * L : (ml + 1) * L, :] = jnp.where(lane < 64, first, second).astype(BF)
    coeff[800:896, :] = jnp.zeros((96, 128), BF)

    def piece(ref, e):
        return ref.at[pl.ds(pl.multiple_of(e * PART, 16), PART)]

    x2 = Exchange(
        "ens", ENS, em, lambda p: piece(coeff, p), lambda m: pooled.at[m],
        coeff.at[pl.ds(0, (ENS - 1) * PART)], pooled.at[pl.ds(0, ENS - 1)], sems2,
    )
    x2.start()
    pooled[em] = piece(coeff, em)[...]
    spread_weights(taps, flipped, wtmp, True)
    x2.arrived()

    small = lax.broadcasted_iota(jnp.int32, (16, 128), 1) % 64

    def other(v):
        return jnp.where(small < 24, pltpu.roll(v, 104, 1), pltpu.roll(v, 24, 1))

    def step(s, carry):
        at = pl.ds(pl.multiple_of(s * 16, 16), 16)
        u = [pooled[a, at, :].astype(F32) for a in range(ENS)]
        w = [jnp.where(small < 48, other(v), 0.0) for v in u]
        goal = target[pl.ds(pl.multiple_of(em * PART + s * 16, 16), 16), :].astype(F32)
        plus = [jnp.zeros((16, 128), F32)] * ENS
        for b in range(ENS):
            turned = jnp.zeros((16, 128), F32)
            for a in range(b):
                one = soft_sign(u[a] - u[b])
                two = soft_sign(u[a] - w[b])
                plus[a] = plus[a] + (one + two)
                plus[b] = plus[b] - one
                turned = turned + two
            plus[b] = plus[b] + soft_sign(u[b] - w[b])
            plus[b] = plus[b] - jnp.where(small < 48, other(turned), 0.0)
        for a in range(ENS):
            grads[a, at, :] = (soft_sign(u[a] - goal) / 16.0 - plus[a] / 240.0).astype(BF)
        return carry

    lax.fori_loop(0, PART // 16, step, 0)
    x3 = Exchange(
        "ens", ENS, em, lambda p: grads.at[p], lambda m: piece(gback, m),
        grads.at[pl.ds(0, ENS - 1)], gback.at[pl.ds(0, (ENS - 1) * PART)], sems3,
    )
    x3.start()
    piece(gback, em)[...] = grads[em]
    mixing = mix_lanes(mix)
    x3.arrived()

    for ml in range(ORDERS):
        s = jnp.dot(leg[ml], gback[ml * L : (ml + 1) * L, :], preferred_element_type=F32)
        for j in range(ROWS):
            rows[:, ml * 6 + j, :] = s[j * 32 : (j + 1) * 32, :]
    send4[...] = rows[...].astype(BF)
    x4 = Exchange(
        "lat", BANDS, me, lambda p: send4.at[p], lambda m: recv4.at[m],
        send4.at[pl.ds(0, BANDS - 1)], recv4.at[pl.ds(0, BANDS - 1)], sems4,
    )
    x4.start()
    recv4[me] = send4[me]
    for ml in range(ORDERS):
        o = jnp.dot(chosen[...], gback[ml * L : (ml + 1) * L, :], preferred_element_type=F32)
        for j in range(5):
            rows[:, ml * 5 + j, :] = o[j * 32 : (j + 1) * 32, :]
    send5[...] = rows[...].astype(BF)
    x5 = Exchange(
        "lat", BANDS, me, lambda p: send5.at[p], lambda m: recv5.at[m],
        send5.at[pl.ds(0, BANDS - 1)], recv5.at[pl.ds(0, BANDS - 1)], sems5,
    )
    recv5[me] = send5[me]

    x4.arrived()
    x5.start()
    rows[...] = jnp.dot(
        recv4[...].reshape(BANDS * 32, 128), mixing, preferred_element_type=F32
    ).reshape(BANDS, 32, 128)
    for i in range(ROWS):
        j = (i % 2) * 3 + i // 2
        q = jnp.concatenate([rows[:, ml * 6 + j, :] for ml in range(ORDERS)], axis=0)
        qt = q.T
        for r in range(2):
            for k in range(2):
                left[r, k, i * 24 : (i + 1) * 24, :] = qt[r * 64 + k * 24 : r * 64 + k * 24 + 24, :]
    halos2 = []
    for k in range(2):
        grad = jnp.dot(left[0, k].astype(BF), table[0:M, :], preferred_element_type=F32)
        grad = grad + jnp.dot(left[1, k].astype(BF), table[M:, :], preferred_element_type=F32)
        for h in range(2):
            hid[k, h] = (grad[h * 72 : (h + 1) * 72] * slope[k, h].astype(F32)).astype(BF)
        pair = halo(hid, low2, high2, halo2_sems, k)
        for copy in pair:
            copy.start()
        halos2.append(pair)

    x5.arrived()
    rows[...] = recv5[...].astype(F32)
    for j in range(5):
        for ml in range(ORDERS):
            turn[pl.ds(ml, BANDS, stride=ORDERS), :] = rows[:, ml * 5 + j, :]
        qt = turn[...].T
        for r in range(2):
            for k in range(2):
                score[k, :, j, r, :] = qt[r * 64 + k * 24 : r * 64 + k * 24 + 24, :]

    for k in range(2):
        ext[0:72, :] = wrapped(hid[k, 0])
        ext[72:144, :] = wrapped(hid[k, 1])
        for h in range(2):
            halos2[k][h].wait_recv()
            fill_halo(low2, high2, k, h)
            out[k, h] = (hid[k, h].astype(F32) + conv_half(flipped, ext, prod, h)).astype(BF)

    for pairs in (halos, halos2):
        for pair in pairs:
            for copy in pair:
                copy.wait_send()
    for exchange in (legx, legx2, x1, x2, x3, x4, x5):
        exchange.done()


HALF = (2, 2, 72, NLON)
CHUNK = (BANDS, 32, 128)


def whole(*args):
    vmem = pl.BlockSpec(memory_space=pltpu.VMEM)
    far = pl.BlockSpec(memory_space=pl.ANY)
    pair = pltpu.SemaphoreType.DMA((2,))
    halo = (2, 72, NLON)
    eighth = (BANDS, 8, 128)
    scratch = [
        (HALF, BF), ((ROWS, M, L), BF), ((2 * M, NLON), BF), ((C, 2, 16, L), BF),
        ((2, 2 * C, 16, 128), F32), ((7, 7, 216), F32), ((2, 144, 384), BF), ((896, 128), BF),
        ((L, L), BF),
        (halo, BF), (halo, BF), (halo, BF), (halo, BF),
        ((2, 504, 216), BF), ((2, 504, 216), BF), ((504, 216), F32),
        ((216, 1536), BF), ((504, 1536), F32), ((144, NLON), BF), (HALF, BF), (HALF, BF),
        ((2, ROWS, M, 128), F32), (eighth, BF), (eighth, BF), ((ENS,) + eighth, BF),
        ((ORDERS, 192, L), BF),
        (CHUNK, F32), (eighth, F32), ((ENS,) + eighth, F32), (CHUNK, BF), (CHUNK, BF),
        ((896, 128), BF), ((ENS, PART, 128), BF), ((ENS, PART, 128), BF), ((896, 128), BF),
        (CHUNK, BF), (CHUNK, BF), (CHUNK, BF), (CHUNK, BF),
        ((2, 2, 144, M), F32), ((M, 128), F32),
    ]
    return pl.pallas_call(
        kernel,
        out_shape=[
            jax.ShapeDtypeStruct(HALF, BF),
            jax.ShapeDtypeStruct((2, C, 5, 2, M), F32),
        ],
        in_specs=[far, far, vmem, far, vmem, far, vmem],
        out_specs=[vmem, vmem],
        scratch_shapes=[pltpu.VMEM(s, d) for s, d in scratch]
        + [pltpu.SemaphoreType.DMA((4,))]
        + [pltpu.SemaphoreType.DMA((4, 2))] * 2
        + [pair] * 7,
        compiler_params=pltpu.CompilerParams(
            vmem_limit_bytes=52 << 20, collective_id=0, has_side_effects=True
        ),
    )(*args)


def local(fields, depth_kernel, mix_weight, legendre, truth, degree_order):
    table = jnp.asarray(wave_table())
    x = jnp.transpose(fields, (0, 2, 1, 3)).reshape(HALF)
    kern = jnp.transpose(depth_kernel, (1, 2, 0))
    out, score = whole(x, legendre, kern, table, mix_weight, truth, degree_order.reshape(1, L))
    grad_fields = jnp.transpose(out.reshape(2, ROWS, C, NLON), (0, 2, 1, 3))
    return grad_fields, jnp.transpose(score, (0, 1, 3, 4, 2))


def solution(mesh):
    placed = (P("ens", None, "lat", None), P(), P(), P("lat", None, None), P(), P())
    return jax.shard_map(
        local,
        mesh=mesh,
        in_specs=placed,
        out_specs=(P("ens", None, "lat", None), P("ens", None, None, None, "lat")),
        check_vma=False,
    )
```

```python
import math

import jax
import jax.numpy as jnp
import ml_dtypes
import numpy as np
from jax import lax
from jax.experimental import pallas as pl
from jax.experimental.pallas import tpu as pltpu
from jax.sharding import PartitionSpec as P

C = 24
NLON = 1440
M = 160
L = 160
BANDS = 32
ROWS = 6
ORDERS = M // BANDS
ENS = 8
PART = 112
BF = jnp.bfloat16
F32 = jnp.float32
MESH = pl.DeviceIdType.MESH


def wave_table():
    m = (np.arange(BANDS)[None, :] * ORDERS + np.arange(ORDERS)[:, None]).reshape(-1)
    angles = (m[:, None] * np.arange(NLON)[None, :] % NLON) * (2.0 * math.pi / NLON)
    both = np.concatenate([np.cos(angles), -np.sin(angles)], axis=0) / math.sqrt(NLON)
    return both.astype(np.float32).astype(ml_dtypes.bfloat16)


def wrapped(x):
    return jnp.concatenate([x[:, NLON - 3 :], x, x[:, :93]], axis=1)


def iota(shape, axis):
    return lax.broadcasted_iota(jnp.int32, shape, axis)


def onehot(hit):
    return jnp.where(hit, 1.0, 0.0).astype(BF)


def tile_taps(kern, taps):
    again = onehot(iota((C, 216), 1) % C == iota((C, 216), 0))
    for p in range(7):
        taps[p] = jnp.dot(kern[p].astype(BF), again, preferred_element_type=F32)


def spread_weights(taps, dst, tmp, flip):
    lane = iota((C, 216), 1)
    same = lane % C == iota((C, 216), 0)
    for h in range(2):
        row = lane // C
        window = lax.rem(row + 3, 9) if h == 0 else row
        masks = [same & (window == g) for g in range(9)]
        for q in range(7):
            tap = []
            for p in range(7):
                a, b = (6 - p, 6 - q) if flip else (p, q)
                tap.append(jnp.broadcast_to(taps[a, b : b + 1, :], (C, 216)))
            for i in range(3):
                total = jnp.zeros((C, 216), F32)
                for p in range(7):
                    total = jnp.where(masks[i + p], tap[p], total)
                tmp[q * 72 + i * 24 : q * 72 + i * 24 + 24, :] = total
        dst[h] = tmp[...].astype(BF)


def place_mix(mix, placing):
    row = iota((144, C), 0)
    tall = lax.dot_general(
        onehot(row % C == iota((144, C), 1)), mix[...], (((1,), (1,)), ((), ())),
        preferred_element_type=F32,
    ).astype(BF)
    for k in range(2):
        wide = onehot(iota((C, 384), 1) % 64 == iota((C, 384), 0) + C * k)
        full = jnp.dot(tall, wide, preferred_element_type=F32)
        same = iota((144, 384), 0) // C == iota((144, 384), 1) // 64
        placing[k] = jnp.where(same, full, 0.0).astype(BF)


def group(v):
    return v // 64 * 2 + v % 64 // C, v % 64 % C


def mix_lanes(mix):
    rk, o = group(iota((128, C), 0))
    tall = jnp.dot(onehot(o == iota((128, C), 1)), mix[...], preferred_element_type=F32).astype(BF)
    rk, c = group(iota((C, 128), 1))
    full = jnp.dot(tall, onehot(c == iota((C, 128), 0)), preferred_element_type=F32)
    a, b = iota((128, 128), 0), iota((128, 128), 1)
    same = (group(a)[0] == group(b)[0]) & (a % 64 < 48) & (b % 64 < 48)
    return jnp.where(same, full, 0.0).astype(BF)


def conv_half(weights, ext, prod, h):
    prod[...] = jnp.dot(weights[h], ext[...], preferred_element_type=F32)
    total = prod[0:72, 0:NLON]
    for q in range(1, 7):
        total = total + prod[q * 72 : (q + 1) * 72, q : q + NLON]
    return total


def soft_sign(gaps):
    return gaps * lax.rsqrt(gaps * gaps + 0.25)


class Exchange:
    def __init__(self, axis, count, me, block, slot, sent, landed, sems):
        self.axis, self.count, self.me = axis, count, me
        self.block, self.slot = block, slot
        self.sent, self.landed, self.sems = sent, landed, sems

    def copy(self, source, target, peer):
        return pltpu.make_async_remote_copy(
            src_ref=source,
            dst_ref=target,
            send_sem=self.sems.at[0],
            recv_sem=self.sems.at[1],
            device_id={self.axis: peer},
            device_id_type=MESH,
        )

    def start(self):
        def step(s, carry):
            peer = lax.rem(self.me + s, self.count)
            self.copy(self.block(peer), self.slot(self.me), peer).start()
            return carry

        lax.fori_loop(1, self.count, step, 0)

    def whole(self):
        return self.copy(self.sent, self.landed, lax.rem(self.me + 1, self.count))

    def arrived(self):
        self.whole().wait_recv()

    def done(self):
        self.whole().wait_send()


def kernel(
    x_hbm, leg_hbm, kern_hbm, table_hbm, mix_hbm, truth, order_hbm,
    out, score,
    x, legl, table, kern, mix, order, window, wide, taps, placing, target, chosen,
    low, high, low2, high2, weights, flipped, wtmp, ext, prod, act, slope, hid,
    legf, legsend, legrecv, legall, leg,
    rows, stage, more, send1, recv1, coeff, pooled, grads, gback, send4, recv4, send5, recv5,
    left, turn,
    load_sems, halo_sems, halo2_sems, leg_sems, leg2_sems, sems1, sems2, sems3, sems4, sems5,
):
    me = lax.axis_index("lat")
    em = lax.axis_index("ens")
    after = lax.rem(me + 1, BANDS)
    before = lax.rem(me + BANDS - 1, BANDS)

    m0 = me * ORDERS
    base = jnp.minimum(m0 // 8 * 8, M - 16)
    loads = [
        pltpu.make_async_copy(source, target_, load_sems.at[n])
        for n, (source, target_) in enumerate(
            [
                (leg_hbm, legl),
                (x_hbm, x),
                (truth.at[:, :, pl.ds(pl.multiple_of(base, 8), 16), :], window),
                (table_hbm, table),
                (kern_hbm, kern),
                (mix_hbm, mix),
                (order_hbm, order),
            ]
        )
    ]
    for load in loads:
        load.start()
    barrier = pltpu.get_barrier_semaphore()

    def greet(axis, count, mine):
        def step(s, carry):
            pl.semaphore_signal(
                barrier, 1, device_id={axis: lax.rem(mine + s, count)}, device_id_type=MESH
            )
            return carry

        lax.fori_loop(1, count, step, 0)

    greet("lat", BANDS, me)
    greet("ens", ENS, em)
    pl.semaphore_wait(barrier, BANDS - 1 + ENS - 1)

    def halo(source, lo, hi, sems, k):
        return (
            pltpu.make_async_remote_copy(
                src_ref=source.at[k, 1], dst_ref=lo.at[k],
                send_sem=sems.at[0, k], recv_sem=sems.at[1, k],
                device_id={"lat": after}, device_id_type=MESH,
            ),
            pltpu.make_async_remote_copy(
                src_ref=source.at[k, 0], dst_ref=hi.at[k],
                send_sem=sems.at[2, k], recv_sem=sems.at[3, k],
                device_id={"lat": before}, device_id_type=MESH,
            ),
        )

    halos = [halo(x_hbm, low, high, halo_sems, k) for k in range(2)]
    for pair in halos:
        for copy in pair:
            copy.start()

    loads[0].wait()
    for i in range(ROWS):
        legf[0, i] = legl[i, :, 0:128].astype(F32)
        legf[1, i] = jnp.concatenate(
            [legl[i, :, 128:L].astype(F32), jnp.zeros((M, 256 - L), F32)], axis=1
        )
    for q in range(4):
        n = jnp.minimum(em * 4 + q, 29)
        for b in range(2):
            stage[:, q * 2 + b, :] = legf[
                b, n // ORDERS, pl.ds(lax.rem(n, ORDERS), BANDS, stride=ORDERS), :
            ]
    legsend[...] = stage[...].astype(BF)
    legx = Exchange(
        "lat", BANDS, me, lambda p: legsend.at[p], lambda m: legrecv.at[m],
        legsend.at[pl.ds(0, BANDS - 1)], legrecv.at[pl.ds(0, BANDS - 1)], leg_sems,
    )
    legx.start()
    legrecv[me] = legsend[me]
    loads[4].wait()
    tile_taps(kern, taps)
    spread_weights(taps, weights, wtmp, False)
    loads[5].wait()
    place_mix(mix, placing)

    def fill_halo(lo, hi, k, h):
        if h == 0:
            edge = wrapped(lo[k].astype(F32))
            ext[144:216, :] = jnp.where(me > 0, edge, 0.0).astype(BF)
        else:
            edge = wrapped(hi[k].astype(F32))
            ext[144:216, :] = jnp.where(me < BANDS - 1, edge, 0.0).astype(BF)

    loads[1].wait()
    loads[3].wait()
    c0 = math.sqrt(2.0 / math.pi)
    spec = jnp.zeros((2 * M, 384), F32)
    for k in range(2):
        ext[0:72, :] = wrapped(x[k, 0])
        ext[72:144, :] = wrapped(x[k, 1])
        for h in range(2):
            halos[k][h].wait_recv()
            fill_halo(low, high, k, h)
            v = x[k, h].astype(F32) + conv_half(weights, ext, prod, h)
            sq = v * v
            t = jnp.tanh(c0 * v * (1.0 + 0.044715 * sq))
            half = 0.5 * (1.0 + t)
            act[h * 72 : (h + 1) * 72, :] = (v * half).astype(BF)
            slope[k, h] = (half + 0.5 * v * (1.0 - t * t) * (c0 * (1.0 + 0.134145 * sq))).astype(BF)
        waves = lax.dot_general(
            table[...], act[...], (((1,), (1,)), ((), ())), preferred_element_type=F32
        ).astype(BF)
        spec = spec + jnp.dot(waves, placing[k], preferred_element_type=F32)
        if k == 0:
            legx.arrived()
            legx2 = Exchange(
                "ens", ENS, em, lambda p: legrecv, lambda m: legall.at[m],
                legall.at[pl.ds(0, ENS - 1)], legall.at[pl.ds(0, ENS - 1)], leg2_sems,
            )
            legx2.start()
            legall[em] = legrecv[...]
    rows[:, 30:32, :] = jnp.zeros((BANDS, 2, 128), F32)
    for a in range(10):
        for t in range(3):
            rows[:, t * 10 + a, :] = spec[a * 32 : (a + 1) * 32, t * 128 : (t + 1) * 128]
    send1[...] = rows[...].astype(BF)
    x1 = Exchange(
        "lat", BANDS, me, lambda p: send1.at[p], lambda m: recv1.at[m],
        send1.at[pl.ds(0, BANDS - 1)], recv1.at[pl.ds(0, BANDS - 1)], sems1,
    )
    x1.start()
    recv1[me] = send1[me]

    loads[2].wait()
    wide[0] = window[:, :, :, 0:128].astype(F32).reshape(2 * C, 16, 128)
    wide[1] = jnp.concatenate(
        [
            window[:, :, :, 128:L].astype(F32).reshape(2 * C, 16, L - 128),
            jnp.zeros((2 * C, 16, 256 - L), F32),
        ],
        axis=2,
    )
    cr, at = iota((2 * C, 128), 0), iota((2 * C, 128), 1)
    spot = onehot((at // 64 == cr % 2) & (at % 64 < 48) & (at % 64 % C == cr // 2))
    for ml in range(ORDERS):
        for b in range(2):
            part = wide[b, :, m0 - base + ml, :].astype(BF)
            t = lax.dot_general(part, spot, (((0,), (0,)), ((), ())), preferred_element_type=F32)
            if b == 0:
                target[ml * L : ml * L + 128, :] = t.astype(BF)
            else:
                target[ml * L + 128 : ml * L + L, :] = t[0 : L - 128].astype(BF)
    target[800:896, :] = jnp.zeros((96, 128), BF)
    place = iota((L, L), 0)
    spots = onehot(iota((L, L), 1) == place % BANDS * 5 + place // BANDS)
    loads[6].wait()
    kept = onehot(place == jnp.broadcast_to(order[...], (L, L)))
    chosen[...] = lax.dot_general(
        spots, kept, (((1,), (1,)), ((), ())), preferred_element_type=F32
    ).astype(BF)

    legx2.arrived()
    more[...] = legall[...].astype(F32)
    for ml in range(ORDERS):
        for i in range(ROWS):
            n, j = i * ORDERS + ml, (i % 2) * 3 + i // 2
            at = slice(j * 32, (j + 1) * 32)
            leg[ml, at, 0:128] = more[n // 4, :, n % 4 * 2, :].astype(BF)
            leg[ml, at, 128:L] = more[n // 4, :, n % 4 * 2 + 1, 0 : L - 128].astype(BF)

    x1.arrived()
    rows[...] = recv1[...].astype(F32)
    lane = lax.broadcasted_iota(jnp.int32, (L, 128), 1)
    for ml in range(ORDERS):
        acc = []
        for r in range(2):
            a = jnp.concatenate(
                [rows[:, t * 10 + r * 5 + ml, :] for t in range(3)], axis=0
            ).astype(BF)
            for par in range(2):
                acc.append(
                    lax.dot_general(
                        leg[ml, par * 96 : (par + 1) * 96, :],
                        a,
                        (((0,), (0,)), ((), ())),
                        preferred_element_type=F32,
                    )
                )
        first = acc[0] + pltpu.roll(acc[1], 64, 1)
        second = pltpu.roll(acc[2], 64, 1) + acc[3]
        coeff[ml * L : (ml + 1) * L, :] = jnp.where(lane < 64, first, second).astype(BF)
    coeff[800:896, :] = jnp.zeros((96, 128), BF)

    def piece(ref, e):
        return ref.at[pl.ds(pl.multiple_of(e * PART, 16), PART)]

    x2 = Exchange(
        "ens", ENS, em, lambda p: piece(coeff, p), lambda m: pooled.at[m],
        coeff.at[pl.ds(0, (ENS - 1) * PART)], pooled.at[pl.ds(0, ENS - 1)], sems2,
    )
    x2.start()
    pooled[em] = piece(coeff, em)[...]
    spread_weights(taps, flipped, wtmp, True)
    x2.arrived()

    small = lax.broadcasted_iota(jnp.int32, (16, 128), 1) % 64

    def other(v):
        return jnp.where(small < 24, pltpu.roll(v, 104, 1), pltpu.roll(v, 24, 1))

    def step(s, carry):
        at = pl.ds(pl.multiple_of(s * 16, 16), 16)
        u = [pooled[a, at, :].astype(F32) for a in range(ENS)]
        w = [jnp.where(small < 48, other(v), 0.0) for v in u]
        goal = target[pl.ds(pl.multiple_of(em * PART + s * 16, 16), 16), :].astype(F32)
        plus = [jnp.zeros((16, 128), F32)] * ENS
        for b in range(ENS):
            turned = jnp.zeros((16, 128), F32)
            for a in range(b):
                one = soft_sign(u[a] - u[b])
                two = soft_sign(u[a] - w[b])
                plus[a] = plus[a] + (one + two)
                plus[b] = plus[b] - one
                turned = turned + two
            plus[b] = plus[b] + soft_sign(u[b] - w[b])
            plus[b] = plus[b] - jnp.where(small < 48, other(turned), 0.0)
        for a in range(ENS):
            grads[a, at, :] = (soft_sign(u[a] - goal) / 16.0 - plus[a] / 240.0).astype(BF)
        return carry

    lax.fori_loop(0, PART // 16, step, 0)
    x3 = Exchange(
        "ens", ENS, em, lambda p: grads.at[p], lambda m: piece(gback, m),
        grads.at[pl.ds(0, ENS - 1)], gback.at[pl.ds(0, (ENS - 1) * PART)], sems3,
    )
    x3.start()
    piece(gback, em)[...] = grads[em]
    mixing = mix_lanes(mix)
    x3.arrived()

    for ml in range(ORDERS):
        s = jnp.dot(leg[ml], gback[ml * L : (ml + 1) * L, :], preferred_element_type=F32)
        for j in range(ROWS):
            rows[:, ml * 6 + j, :] = s[j * 32 : (j + 1) * 32, :]
    send4[...] = rows[...].astype(BF)
    x4 = Exchange(
        "lat", BANDS, me, lambda p: send4.at[p], lambda m: recv4.at[m],
        send4.at[pl.ds(0, BANDS - 1)], recv4.at[pl.ds(0, BANDS - 1)], sems4,
    )
    x4.start()
    recv4[me] = send4[me]
    for ml in range(ORDERS):
        o = jnp.dot(chosen[...], gback[ml * L : (ml + 1) * L, :], preferred_element_type=F32)
        for j in range(5):
            rows[:, ml * 5 + j, :] = o[j * 32 : (j + 1) * 32, :]
    send5[...] = rows[...].astype(BF)
    x5 = Exchange(
        "lat", BANDS, me, lambda p: send5.at[p], lambda m: recv5.at[m],
        send5.at[pl.ds(0, BANDS - 1)], recv5.at[pl.ds(0, BANDS - 1)], sems5,
    )
    recv5[me] = send5[me]

    x4.arrived()
    x5.start()
    rows[...] = jnp.dot(
        recv4[...].reshape(BANDS * 32, 128), mixing, preferred_element_type=F32
    ).reshape(BANDS, 32, 128)
    for i in range(ROWS):
        j = (i % 2) * 3 + i // 2
        q = jnp.concatenate([rows[:, ml * 6 + j, :] for ml in range(ORDERS)], axis=0)
        qt = q.T
        for r in range(2):
            for k in range(2):
                left[r, k, i * 24 : (i + 1) * 24, :] = qt[r * 64 + k * 24 : r * 64 + k * 24 + 24, :]
    halos2 = []
    for k in range(2):
        grad = jnp.dot(left[0, k].astype(BF), table[0:M, :], preferred_element_type=F32)
        grad = grad + jnp.dot(left[1, k].astype(BF), table[M:, :], preferred_element_type=F32)
        for h in range(2):
            hid[k, h] = (grad[h * 72 : (h + 1) * 72] * slope[k, h].astype(F32)).astype(BF)
        pair = halo(hid, low2, high2, halo2_sems, k)
        for copy in pair:
            copy.start()
        halos2.append(pair)

    for k in range(2):
        ext[0:72, :] = wrapped(hid[k, 0])
        ext[72:144, :] = wrapped(hid[k, 1])
        for h in range(2):
            halos2[k][h].wait_recv()
            fill_halo(low2, high2, k, h)
            out[k, h] = (hid[k, h].astype(F32) + conv_half(flipped, ext, prod, h)).astype(BF)
        if k == 0:
            x5.arrived()
            rows[...] = recv5[...].astype(F32)
            for j in range(5):
                for ml in range(ORDERS):
                    turn[pl.ds(ml, BANDS, stride=ORDERS), :] = rows[:, ml * 5 + j, :]
                qt = turn[...].T
                for r in range(2):
                    for k in range(2):
                        score[k, :, j, r, :] = qt[r * 64 + k * 24 : r * 64 + k * 24 + 24, :]

    for pairs in (halos, halos2):
        for pair in pairs:
            for copy in pair:
                copy.wait_send()
    for exchange in (legx, legx2, x1, x2, x3, x4, x5):
        exchange.done()


HALF = (2, 2, 72, NLON)
CHUNK = (BANDS, 32, 128)


def whole(*args):
    vmem = pl.BlockSpec(memory_space=pltpu.VMEM)
    far = pl.BlockSpec(memory_space=pltpu.HBM)
    pair = pltpu.SemaphoreType.DMA((2,))
    halo = (2, 72, NLON)
    eighth = (BANDS, 8, 128)
    scratch = [
        (HALF, BF), ((ROWS, M, L), BF), ((2 * M, NLON), BF), ((7, 7, C), F32), ((C, C), BF),
        ((1, L), jnp.int32), ((C, 2, 16, L), BF),
        ((2, 2 * C, 16, 128), F32), ((7, 7, 216), F32), ((2, 144, 384), BF), ((896, 128), BF),
        ((L, L), BF),
        (halo, BF), (halo, BF), (halo, BF), (halo, BF),
        ((2, 504, 216), BF), ((2, 504, 216), BF), ((504, 216), F32),
        ((216, 1536), BF), ((504, 1536), F32), ((144, NLON), BF), (HALF, BF), (HALF, BF),
        ((2, ROWS, M, 128), F32), (eighth, BF), (eighth, BF), ((ENS,) + eighth, BF),
        ((ORDERS, 192, L), BF),
        (CHUNK, F32), (eighth, F32), ((ENS,) + eighth, F32), (CHUNK, BF), (CHUNK, BF),
        ((896, 128), BF), ((ENS, PART, 128), BF), ((ENS, PART, 128), BF), ((896, 128), BF),
        (CHUNK, BF), (CHUNK, BF), (CHUNK, BF), (CHUNK, BF),
        ((2, 2, 144, M), F32), ((M, 128), F32),
    ]
    return pl.pallas_call(
        kernel,
        out_shape=[
            jax.ShapeDtypeStruct(HALF, BF),
            jax.ShapeDtypeStruct((2, C, 5, 2, M), F32),
        ],
        in_specs=[far] * len(args),
        out_specs=[vmem, vmem],
        scratch_shapes=[pltpu.VMEM(s, d) for s, d in scratch]
        + [pltpu.SemaphoreType.DMA((7,))]
        + [pltpu.SemaphoreType.DMA((4, 2))] * 2
        + [pair] * 7,
        compiler_params=pltpu.CompilerParams(
            vmem_limit_bytes=52 << 20, collective_id=0, has_side_effects=True
        ),
    )(*args)


def local(fields, depth_kernel, mix_weight, legendre, truth, degree_order):
    table = jnp.asarray(wave_table())
    x = jnp.transpose(fields, (0, 2, 1, 3)).reshape(HALF)
    kern = jnp.transpose(depth_kernel, (1, 2, 0))
    out, score = whole(x, legendre, kern, table, mix_weight, truth, degree_order.reshape(1, L))
    grad_fields = jnp.transpose(out.reshape(2, ROWS, C, NLON), (0, 2, 1, 3))
    return grad_fields, jnp.transpose(score, (0, 1, 3, 4, 2))


def solution(mesh):
    placed = (P("ens", None, "lat", None), P(), P(), P("lat", None, None), P(), P())
    return jax.shard_map(
        local,
        mesh=mesh,
        in_specs=placed,
        out_specs=(P("ens", None, "lat", None), P("ens", None, None, None, "lat")),
        check_vma=False,
    )
```

```python
import math

import jax
import jax.numpy as jnp
import ml_dtypes
import numpy as np
from jax import lax
from jax.experimental import pallas as pl
from jax.experimental.pallas import tpu as pltpu
from jax.sharding import PartitionSpec as P

C = 24
NLON = 1440
M = 160
L = 160
BANDS = 32
ROWS = 6
ORDERS = M // BANDS
ENS = 8
WORLD = ENS * BANDS
SHARE = C // ENS
BF = jnp.bfloat16
F32 = jnp.float32
MESH = pl.DeviceIdType.MESH


def wave_table():
    m = (np.arange(BANDS)[None, :] * ORDERS + np.arange(ORDERS)[:, None]).reshape(-1)
    angles = (m[:, None] * np.arange(NLON)[None, :] % NLON) * (2.0 * math.pi / NLON)
    both = np.concatenate([np.cos(angles), -np.sin(angles)], axis=0) / math.sqrt(NLON)
    return both.astype(np.float32).astype(ml_dtypes.bfloat16)


def wrapped(x):
    return jnp.concatenate([x[:, NLON - 3 :], x, x[:, :93]], axis=1)


def iota(shape, axis):
    return lax.broadcasted_iota(jnp.int32, shape, axis)


def onehot(hit):
    return jnp.where(hit, 1.0, 0.0).astype(BF)


def tile_taps(kern, taps):
    again = onehot(iota((C, 216), 1) % C == iota((C, 216), 0))
    for p in range(7):
        taps[p] = jnp.dot(kern[p].astype(BF), again, preferred_element_type=F32)


def spread_weights(taps, dst, tmp, flip):
    lane = iota((C, 216), 1)
    same = lane % C == iota((C, 216), 0)
    for h in range(2):
        row = lane // C
        window = lax.rem(row + 3, 9) if h == 0 else row
        masks = [same & (window == g) for g in range(9)]
        for q in range(7):
            tap = []
            for p in range(7):
                a, b = (6 - p, 6 - q) if flip else (p, q)
                tap.append(jnp.broadcast_to(taps[a, b : b + 1, :], (C, 216)))
            for i in range(3):
                total = jnp.zeros((C, 216), F32)
                for p in range(7):
                    total = jnp.where(masks[i + p], tap[p], total)
                tmp[q * 72 + i * 24 : q * 72 + i * 24 + 24, :] = total
        dst[h] = tmp[...].astype(BF)


def place_mix(mix, placing):
    row = iota((144, C), 0)
    tall = lax.dot_general(
        onehot(row % C == iota((144, C), 1)), mix[...], (((1,), (1,)), ((), ())),
        preferred_element_type=F32,
    ).astype(BF)
    lane = iota((C, 384), 1)
    q = lane % 16
    channel = lane % 128 // 16 * SHARE + q % 3
    full_lane = iota((144, 384), 1)
    line = full_lane // 128 * 2 + full_lane % 16 // 6
    same = (iota((144, 384), 0) // C == line) & (full_lane % 16 < 12)
    for k in range(2):
        wide = onehot((channel == iota((C, 384), 0)) & (q % 6 // 3 == k))
        full = jnp.dot(tall, wide, preferred_element_type=F32)
        placing[k] = jnp.where(same, full, 0.0).astype(BF)


def gather_lanes(dst):
    for a in range(10):
        r, ml = a // ORDERS, a % ORDERS
        row = iota((128, 1), 0)
        q = row % 16
        spot = row // 16 * 128 + q // 6 * 60 + ml * 12 + r * 6 + q % 6
        spot = jnp.where(q < 12, spot, -1)
        dst[a * 128 : (a + 1) * 128, :] = onehot(iota((128, 1024), 1) == spot)


def mix_lanes(mix, dst):
    row, lane = iota((128, 1), 0), iota((1, 1280), 1)
    par, ml, r, k = row // 60, row % 60 // 12, row % 12 // 6, row % 6 // 3
    code = jnp.where(row < 120, ((r * 5 + ml) * 2 + par) * 2 + k, -1)
    kc = lane % 64
    seen = jnp.where(kc < 48, lane // 64 * 2 + kc // C, -2)
    same = code == seen
    wide = onehot(iota((C, 1280), 1) % 64 % C == iota((C, 1280), 0))
    for e in range(ENS):
        pick = onehot(iota((128, C), 1) == e * SHARE + iota((128, C), 0) % 3)
        tall = jnp.dot(pick, mix[...], preferred_element_type=F32).astype(BF)
        full = jnp.dot(tall, wide, preferred_element_type=F32)
        dst[e * 128 : (e + 1) * 128, :] = jnp.where(same, full, 0.0).astype(BF)


def scatter_lanes(dst):
    row = iota((128, 1), 0)
    for e in range(ENS):
        ml, r, k = row // 12, row % 12 // 6, row % 6 // 3
        spot = ml * 128 + r * 64 + k * C + e * SHARE + row % 3
        spot = jnp.where(row < 60, spot, -1)
        dst[e * 128 : (e + 1) * 128, :] = onehot(iota((128, 640), 1) == spot)


def conv_half(weights, ext, prod, h):
    prod[...] = jnp.dot(weights[h], ext[...], preferred_element_type=F32)
    total = prod[0:72, 0:NLON]
    for q in range(1, 7):
        total = total + prod[q * 72 : (q + 1) * 72, q : q + NLON]
    return total


def soft_sign(gaps):
    return gaps * lax.rsqrt(gaps * gaps + 0.25)


class Exchange:
    def __init__(self, axis, count, me, block, slot, sent, landed, sems):
        self.axis, self.count, self.me = axis, count, me
        self.block, self.slot = block, slot
        self.sent, self.landed, self.sems = sent, landed, sems

    def device(self, peer):
        if self.axis is None:
            return {"ens": peer // BANDS, "lat": lax.rem(peer, BANDS)}
        return {self.axis: peer}

    def copy(self, source, target, peer):
        return pltpu.make_async_remote_copy(
            src_ref=source,
            dst_ref=target,
            send_sem=self.sems.at[0],
            recv_sem=self.sems.at[1],
            device_id=self.device(peer),
            device_id_type=MESH,
        )

    def start(self):
        def step(s, carry):
            peer = lax.rem(self.me + s, self.count)
            self.copy(self.block(peer), self.slot(self.me), peer).start()
            return carry

        lax.fori_loop(1, self.count, step, 0)

    def whole(self):
        return self.copy(self.sent, self.landed, lax.rem(self.me + 1, self.count))

    def arrived(self):
        self.whole().wait_recv()

    def done(self):
        self.whole().wait_send()


def kernel(
    x_hbm, leg_hbm, kern_hbm, table_hbm, mix_hbm, truth, order_hbm,
    out, score,
    x, legl, table, kern, mix, order, window, wide, taps, placing, target, chosen,
    low, high, low2, high2, weights, flipped, wtmp, ext, prod, act, slope, hid,
    legf, legsend, legrecv, legall, leg,
    flat, stage, more, send1, recv1, coeff, grads, send4, recv4, send5, recv5,
    left, turn, regroup, mixing, regroup5,
    load_sems, halo_sems, halo2_sems, leg_sems, leg2_sems, sems1, sems4, sems5, entered,
):
    me = lax.axis_index("lat")
    em = lax.axis_index("ens")
    after = lax.rem(me + 1, BANDS)
    before = lax.rem(me + BANDS - 1, BANDS)

    m0 = me * ORDERS
    base = jnp.minimum(m0 // 8 * 8, M - 16)
    loads = [
        pltpu.make_async_copy(source, target_, load_sems.at[n])
        for n, (source, target_) in enumerate(
            [
                (leg_hbm, legl),
                (x_hbm, x),
                (truth.at[:, :, pl.ds(pl.multiple_of(base, 8), 16), :], window),
                (table_hbm, table),
                (kern_hbm, kern),
                (mix_hbm, mix),
                (order_hbm, order),
            ]
        )
    ]
    for load in loads:
        load.start()
    barrier = pltpu.get_barrier_semaphore()

    def greet(axis, count, mine):
        def step(s, carry):
            pl.semaphore_signal(
                barrier, 1, device_id={axis: lax.rem(mine + s, count)}, device_id_type=MESH
            )
            return carry

        lax.fori_loop(1, count, step, 0)

    greet("lat", BANDS, me)
    greet("ens", ENS, em)
    pl.semaphore_wait(barrier, BANDS - 1 + ENS - 1)

    def tell(s, carry):
        pl.semaphore_signal(
            entered, 1, device_id={"ens": lax.rem(em + s, ENS)}, device_id_type=MESH
        )
        return carry

    lax.fori_loop(1, ENS, tell, 0)

    def halo(source, lo, hi, sems, k):
        return (
            pltpu.make_async_remote_copy(
                src_ref=source.at[k, 1], dst_ref=lo.at[k],
                send_sem=sems.at[0, k], recv_sem=sems.at[1, k],
                device_id={"lat": after}, device_id_type=MESH,
            ),
            pltpu.make_async_remote_copy(
                src_ref=source.at[k, 0], dst_ref=hi.at[k],
                send_sem=sems.at[2, k], recv_sem=sems.at[3, k],
                device_id={"lat": before}, device_id_type=MESH,
            ),
        )

    halos = [halo(x_hbm, low, high, halo_sems, k) for k in range(2)]
    for pair in halos:
        for copy in pair:
            copy.start()

    loads[0].wait()
    for i in range(ROWS):
        legf[0, i] = legl[i, :, 0:128].astype(F32)
        legf[1, i] = jnp.concatenate(
            [legl[i, :, 128:L].astype(F32), jnp.zeros((M, 256 - L), F32)], axis=1
        )
    for q in range(4):
        n = jnp.minimum(em * 4 + q, 29)
        for b in range(2):
            stage[:, q * 2 + b, :] = legf[
                b, n // ORDERS, pl.ds(lax.rem(n, ORDERS), BANDS, stride=ORDERS), :
            ]
    legsend[...] = stage[...].astype(BF)
    legx = Exchange(
        "lat", BANDS, me, lambda p: legsend.at[p], lambda m: legrecv.at[m],
        legsend.at[pl.ds(0, BANDS - 1)], legrecv.at[pl.ds(0, BANDS - 1)], leg_sems,
    )
    legx.start()
    legrecv[me] = legsend[me]
    loads[4].wait()
    tile_taps(kern, taps)
    spread_weights(taps, weights, wtmp, False)
    loads[5].wait()
    place_mix(mix, placing)
    gather_lanes(regroup)

    def fill_halo(lo, hi, k, h):
        if h == 0:
            edge = wrapped(lo[k].astype(F32))
            ext[144:216, :] = jnp.where(me > 0, edge, 0.0).astype(BF)
        else:
            edge = wrapped(hi[k].astype(F32))
            ext[144:216, :] = jnp.where(me < BANDS - 1, edge, 0.0).astype(BF)

    loads[1].wait()
    loads[3].wait()
    c0 = math.sqrt(2.0 / math.pi)
    spec = jnp.zeros((2 * M, 384), F32)
    for k in range(2):
        ext[0:72, :] = wrapped(x[k, 0])
        ext[72:144, :] = wrapped(x[k, 1])
        for h in range(2):
            halos[k][h].wait_recv()
            fill_halo(low, high, k, h)
            v = x[k, h].astype(F32) + conv_half(weights, ext, prod, h)
            sq = v * v
            t = jnp.tanh(c0 * v * (1.0 + 0.044715 * sq))
            half = 0.5 * (1.0 + t)
            act[h * 72 : (h + 1) * 72, :] = (v * half).astype(BF)
            slope[k, h] = (half + 0.5 * v * (1.0 - t * t) * (c0 * (1.0 + 0.134145 * sq))).astype(BF)
        waves = lax.dot_general(
            table[...], act[...], (((1,), (1,)), ((), ())), preferred_element_type=F32
        ).astype(BF)
        spec = spec + jnp.dot(waves, placing[k], preferred_element_type=F32)
        if k == 0:
            legx.arrived()
            legx2 = Exchange(
                "ens", ENS, em, lambda p: legrecv, lambda m: legall.at[m],
                legall.at[pl.ds(0, ENS - 1)], legall.at[pl.ds(0, ENS - 1)], leg2_sems,
            )
            legx2.start()
            legall[em] = legrecv[...]
    spec = spec.astype(BF)
    lined = jnp.concatenate(
        [
            jnp.concatenate(
                [spec[a * 32 : (a + 1) * 32, t * 128 : (t + 1) * 128] for a in range(10)], axis=1
            )
            for t in range(3)
        ],
        axis=0,
    )
    lined = jnp.dot(lined, regroup[...], preferred_element_type=F32)

    def tile(e, t):
        return pl.ds(e * 128 + t, BANDS, stride=4)

    for e in range(ENS):
        for t in range(3):
            flat[tile(e, t), :] = lined[t * 32 : (t + 1) * 32, e * 128 : (e + 1) * 128]
        flat[tile(e, 3), :] = jnp.zeros((BANDS, 128), F32)
    send1[...] = flat[...].reshape(WORLD, 4, 128).astype(BF)
    self_at = em * BANDS + me

    def swap_all(send, recv, sems):
        exchange = Exchange(
            None, WORLD, self_at, lambda p: send.at[p], lambda m: recv.at[m],
            send.at[pl.ds(0, WORLD - 1)], recv.at[pl.ds(0, WORLD - 1)], sems,
        )
        return exchange

    pl.semaphore_wait(entered, ENS - 1)
    x1 = swap_all(send1, recv1, sems1)
    x1.start()
    recv1[self_at] = send1[self_at]

    loads[2].wait()
    wide[0] = window[:, :, :, 0:128].astype(F32).reshape(2 * C, 16, 128)
    wide[1] = jnp.concatenate(
        [
            window[:, :, :, 128:L].astype(F32).reshape(2 * C, 16, L - 128),
            jnp.zeros((2 * C, 16, 256 - L), F32),
        ],
        axis=2,
    )
    lane = iota((80, 128), 1)

    def folded(v):
        return jnp.where(
            lane % 64 < 60, jnp.where(lane < 64, v[0:80], pltpu.roll(v[80:160], 64, 1)), 0.0
        )

    cr, at = iota((2 * C, 128), 0), iota((2 * C, 128), 1)
    mine = (cr // 2 == em * SHARE + at % 3) & (cr % 2 == at % 12 // 6)
    goal0, goal1 = jnp.zeros((128, 128), F32), jnp.zeros((128, 128), F32)
    for ml in range(ORDERS):
        spot = onehot(mine & (at // 12 == ml))
        for b in range(2):
            part = wide[b, :, m0 - base + ml, :].astype(BF)
            t = lax.dot_general(part, spot, (((0,), (0,)), ((), ())), preferred_element_type=F32)
            if b == 0:
                goal0 = goal0 + t
            else:
                goal1 = goal1 + t
    target[...] = folded(jnp.concatenate([goal0, goal1[0 : L - 128]], axis=0))
    place = iota((L, L), 0)
    spots = onehot(iota((L, L), 1) == place % BANDS * 5 + place // BANDS)
    loads[6].wait()
    kept = onehot(place == jnp.broadcast_to(order[...], (L, L)))
    chosen[...] = lax.dot_general(
        spots, kept, (((1,), (1,)), ((), ())), preferred_element_type=F32
    ).astype(BF)

    legx2.arrived()
    more[...] = legall[...].astype(F32)
    for ml in range(ORDERS):
        for i in range(ROWS):
            n, j = i * ORDERS + ml, (i % 2) * 3 + i // 2
            at = slice(j * 32, (j + 1) * 32)
            leg[ml, at, 0:128] = more[n // 4, :, n % 4 * 2, :].astype(BF)
            leg[ml, at, 128:L] = more[n // 4, :, n % 4 * 2 + 1, 0 : L - 128].astype(BF)
    spread_weights(taps, flipped, wtmp, True)
    mix_lanes(mix, mixing)
    scatter_lanes(regroup5)

    x1.arrived()

    def arranged(recv):
        flat[...] = recv[...].astype(F32).reshape(WORLD * 4, 128)
        return jnp.concatenate(
            [
                jnp.concatenate([flat[tile(e, t), :] for e in range(ENS)], axis=1)
                for t in range(3)
            ],
            axis=0,
        )

    waves = arranged(recv1)
    kind = iota((96, 1024), 1) % 128 // 12
    acc = jnp.zeros((L, 1024), F32)
    for ml in range(ORDERS):
        both = jnp.concatenate(
            [jnp.where(kind == ml, waves, 0.0), jnp.where(kind == ml + 5, waves, 0.0)], axis=0
        ).astype(BF)
        acc = acc + lax.dot_general(
            leg[ml], both, (((0,), (0,)), ((), ())), preferred_element_type=F32
        )
    for e in range(ENS):
        v = acc[:, e * 128 : (e + 1) * 128]
        coeff[e] = folded(v + pltpu.roll(v, 68, 1))

    small = iota((16, 128), 1) % 64

    def other(v):
        return jnp.where(small % 6 < 3, pltpu.roll(v, 125, 1), pltpu.roll(v, 3, 1))

    def step(s, carry):
        at = pl.ds(pl.multiple_of(s * 16, 16), 16)
        u = [coeff[a, at, :] for a in range(ENS)]
        w = [jnp.where(small < 60, other(v), 0.0) for v in u]
        goal = target[at, :]
        plus = [jnp.zeros((16, 128), F32)] * ENS
        for b in range(ENS):
            turned = jnp.zeros((16, 128), F32)
            for a in range(b):
                one = soft_sign(u[a] - u[b])
                two = soft_sign(u[a] - w[b])
                plus[a] = plus[a] + (one + two)
                plus[b] = plus[b] - one
                turned = turned + two
            plus[b] = plus[b] + soft_sign(u[b] - w[b])
            plus[b] = plus[b] - jnp.where(small < 60, other(turned), 0.0)
        for a in range(ENS):
            coeff[a, at, :] = soft_sign(u[a] - goal) / 16.0 - plus[a] / 240.0
        return carry

    lax.fori_loop(0, 5, step, 0)
    for e in range(ENS):
        g = coeff[e]
        tall = jnp.concatenate([g, pltpu.roll(g, 64, 1)], axis=0)
        grads[:, e * 128 : (e + 1) * 128] = jnp.where(iota((L, 128), 1) < 60, tall, 0.0).astype(BF)
    kind = iota((L, 1024), 1) % 128 // 12
    acc = jnp.zeros((192, 1024), F32)
    for ml in range(ORDERS):
        g = jnp.where(kind == ml, grads[...].astype(F32), 0.0).astype(BF)
        acc = acc + jnp.dot(leg[ml], g, preferred_element_type=F32)
    for e in range(ENS):
        for t in range(3):
            even = acc[t * 32 : (t + 1) * 32, e * 128 : (e + 1) * 128]
            odd = acc[96 + t * 32 : 96 + (t + 1) * 32, e * 128 : (e + 1) * 128]
            flat[tile(e, t), :] = even + pltpu.roll(odd, 60, 1)
    send4[...] = flat[...].reshape(WORLD, 4, 128).astype(BF)
    x4 = swap_all(send4, recv4, sems4)
    x4.start()
    recv4[self_at] = send4[self_at]
    o = jnp.dot(chosen[...], grads[...], preferred_element_type=F32)
    for e in range(ENS):
        part = [o[j * 32 : (j + 1) * 32, e * 128 : (e + 1) * 128] for j in range(5)]
        for t in range(2):
            flat[tile(e, t), :] = part[2 * t] + pltpu.roll(part[2 * t + 1], 64, 1)
        flat[tile(e, 2), :] = part[4]
    send5[...] = flat[...].reshape(WORLD, 4, 128).astype(BF)
    x5 = swap_all(send5, recv5, sems5)
    recv5[self_at] = send5[self_at]

    x4.arrived()
    x5.start()
    lined = jnp.dot(arranged(recv4).astype(BF), mixing[...], preferred_element_type=F32)
    for t in range(3):
        for r in range(2):
            q = jnp.concatenate(
                [
                    lined[t * 32 : (t + 1) * 32, (r * 5 + ml) * 128 : (r * 5 + ml + 1) * 128]
                    for ml in range(ORDERS)
                ],
                axis=0,
            )
            qt = q.T
            for par in range(2):
                for k in range(2):
                    at = par * 64 + k * C
                    i = 2 * t + par
                    left[r, k, i * C : (i + 1) * C, :] = qt[at : at + C, :]
    halos2 = []
    for k in range(2):
        grad = jnp.dot(left[0, k].astype(BF), table[0:M, :], preferred_element_type=F32)
        grad = grad + jnp.dot(left[1, k].astype(BF), table[M:, :], preferred_element_type=F32)
        for h in range(2):
            hid[k, h] = (grad[h * 72 : (h + 1) * 72] * slope[k, h].astype(F32)).astype(BF)
        pair = halo(hid, low2, high2, halo2_sems, k)
        for copy in pair:
            copy.start()
        halos2.append(pair)

    for k in range(2):
        ext[0:72, :] = wrapped(hid[k, 0])
        ext[72:144, :] = wrapped(hid[k, 1])
        for h in range(2):
            halos2[k][h].wait_recv()
            fill_halo(low2, high2, k, h)
            out[k, h] = (hid[k, h].astype(F32) + conv_half(flipped, ext, prod, h)).astype(BF)
        if k == 0:
            x5.arrived()
            got = arranged(recv5)
            lined = []
            for j in range(5):
                v = got[j // 2 * 32 : j // 2 * 32 + 32]
                if j % 2:
                    v = jnp.concatenate(
                        [pltpu.roll(v[:, e * 128 : (e + 1) * 128], 64, 1) for e in range(ENS)], axis=1
                    )
                lined.append(v)
            lined = jnp.concatenate(lined, axis=0).astype(BF)
            lined = jnp.dot(lined, regroup5[...], preferred_element_type=F32)
            for j in range(5):
                for ml in range(ORDERS):
                    turn[pl.ds(ml, BANDS, stride=ORDERS), :] = lined[
                        j * 32 : (j + 1) * 32, ml * 128 : (ml + 1) * 128
                    ]
                qt = turn[...].T
                for r in range(2):
                    for k in range(2):
                        score[k, :, j, r, :] = qt[r * 64 + k * 24 : r * 64 + k * 24 + 24, :]

    for pairs in (halos, halos2):
        for pair in pairs:
            for copy in pair:
                copy.wait_send()
    for exchange in (legx, legx2, x1, x4, x5):
        exchange.done()


HALF = (2, 2, 72, NLON)
CHUNK = (WORLD, 4, 128)


def whole(*args):
    vmem = pl.BlockSpec(memory_space=pltpu.VMEM)
    far = pl.BlockSpec(memory_space=pltpu.HBM)
    pair = pltpu.SemaphoreType.DMA((2,))
    halo = (2, 72, NLON)
    eighth = (BANDS, 8, 128)
    scratch = [
        (HALF, BF), ((ROWS, M, L), BF), ((2 * M, NLON), BF), ((7, 7, C), F32), ((C, C), BF),
        ((1, L), jnp.int32), ((C, 2, 16, L), BF),
        ((2, 2 * C, 16, 128), F32), ((7, 7, 216), F32), ((2, 144, 384), BF), ((80, 128), F32),
        ((L, L), BF),
        (halo, BF), (halo, BF), (halo, BF), (halo, BF),
        ((2, 504, 216), BF), ((2, 504, 216), BF), ((504, 216), F32),
        ((216, 1536), BF), ((504, 1536), F32), ((144, NLON), BF), (HALF, BF), (HALF, BF),
        ((2, ROWS, M, 128), F32), (eighth, BF), (eighth, BF), ((ENS,) + eighth, BF),
        ((ORDERS, 192, L), BF),
        ((WORLD * 4, 128), F32), (eighth, F32), ((ENS,) + eighth, F32), (CHUNK, BF), (CHUNK, BF),
        ((ENS, 80, 128), F32), ((L, 1024), BF), (CHUNK, BF), (CHUNK, BF), (CHUNK, BF), (CHUNK, BF),
        ((2, 2, 144, M), F32), ((M, 128), F32),
        ((1280, 1024), BF), ((1024, 1280), BF), ((1024, 640), BF),
    ]
    return pl.pallas_call(
        kernel,
        out_shape=[
            jax.ShapeDtypeStruct(HALF, BF),
            jax.ShapeDtypeStruct((2, C, 5, 2, M), F32),
        ],
        in_specs=[far] * len(args),
        out_specs=[vmem, vmem],
        scratch_shapes=[pltpu.VMEM(s, d) for s, d in scratch]
        + [pltpu.SemaphoreType.DMA((7,))]
        + [pltpu.SemaphoreType.DMA((4, 2))] * 2
        + [pair] * 5
        + [pltpu.SemaphoreType.REGULAR],
        compiler_params=pltpu.CompilerParams(
            vmem_limit_bytes=62 << 20, collective_id=0, has_side_effects=True
        ),
    )(*args)


def local(fields, depth_kernel, mix_weight, legendre, truth, degree_order):
    table = jnp.asarray(wave_table())
    x = jnp.transpose(fields, (0, 2, 1, 3)).reshape(HALF)
    kern = jnp.transpose(depth_kernel, (1, 2, 0))
    out, score = whole(x, legendre, kern, table, mix_weight, truth, degree_order.reshape(1, L))
    grad_fields = jnp.transpose(out.reshape(2, ROWS, C, NLON), (0, 2, 1, 3))
    return grad_fields, jnp.transpose(score, (0, 1, 3, 4, 2))


def solution(mesh):
    placed = (P("ens", None, "lat", None), P(), P(), P("lat", None, None), P(), P())
    return jax.shard_map(
        local,
        mesh=mesh,
        in_specs=placed,
        out_specs=(P("ens", None, "lat", None), P("ens", None, None, None, "lat")),
        check_vma=False,
    )
```

```python
import math

import jax
import jax.numpy as jnp
import ml_dtypes
import numpy as np
from jax import lax
from jax.experimental import pallas as pl
from jax.experimental.pallas import tpu as pltpu
from jax.sharding import PartitionSpec as P

C = 24
NLON = 1440
M = 160
L = 160
BANDS = 32
ROWS = 6
ORDERS = M // BANDS
ENS = 8
WORLD = ENS * BANDS
SHARE = C // ENS
BF = jnp.bfloat16
F32 = jnp.float32
MESH = pl.DeviceIdType.MESH


def wave_table():
    m = (np.arange(BANDS)[None, :] * ORDERS + np.arange(ORDERS)[:, None]).reshape(-1)
    angles = (m[:, None] * np.arange(NLON)[None, :] % NLON) * (2.0 * math.pi / NLON)
    both = np.concatenate([np.cos(angles), -np.sin(angles)], axis=0) / math.sqrt(NLON)
    return both.astype(np.float32).astype(ml_dtypes.bfloat16)


def wrapped(x):
    return jnp.concatenate([x[:, NLON - 3 :], x, x[:, :93]], axis=1)


def iota(shape, axis):
    return lax.broadcasted_iota(jnp.int32, shape, axis)


def onehot(hit):
    return jnp.where(hit, 1.0, 0.0).astype(BF)


def tile_taps(kern, taps):
    again = onehot(iota((C, 216), 1) % C == iota((C, 216), 0))
    for p in range(7):
        taps[p] = jnp.dot(kern[p].astype(BF), again, preferred_element_type=F32)


def spread_weights(taps, dst, tmp, flip):
    lane = iota((C, 216), 1)
    same = lane % C == iota((C, 216), 0)
    for h in range(2):
        row = lane // C
        window = lax.rem(row + 3, 9) if h == 0 else row
        masks = [same & (window == g) for g in range(9)]
        for q in range(7):
            tap = []
            for p in range(7):
                a, b = (6 - p, 6 - q) if flip else (p, q)
                tap.append(jnp.broadcast_to(taps[a, b : b + 1, :], (C, 216)))
            for i in range(3):
                total = jnp.zeros((C, 216), F32)
                for p in range(7):
                    total = jnp.where(masks[i + p], tap[p], total)
                tmp[q * 72 + i * 24 : q * 72 + i * 24 + 24, :] = total
        dst[h] = tmp[...].astype(BF)


def place_mix(mix, placing):
    row = iota((144, C), 0)
    tall = lax.dot_general(
        onehot(row % C == iota((144, C), 1)), mix[...], (((1,), (1,)), ((), ())),
        preferred_element_type=F32,
    ).astype(BF)
    lane = iota((C, 384), 1)
    q = lane % 16
    channel = lane % 128 // 16 * SHARE + q % 3
    full_lane = iota((144, 384), 1)
    line = full_lane // 128 * 2 + full_lane % 16 // 6
    same = (iota((144, 384), 0) // C == line) & (full_lane % 16 < 12)
    for k in range(2):
        wide = onehot((channel == iota((C, 384), 0)) & (q % 6 // 3 == k))
        full = jnp.dot(tall, wide, preferred_element_type=F32)
        placing[k] = jnp.where(same, full, 0.0).astype(BF)


def gather_lanes():
    a, e, q = np.meshgrid(np.arange(10), np.arange(ENS), np.arange(16), indexing="ij")
    spot = e * 128 + q // 6 * 60 + a % ORDERS * 12 + a // ORDERS * 6 + q % 6
    spot = np.where(q < 12, spot, -1).reshape(-1, 1)
    return (np.arange(1024) == spot).astype(ml_dtypes.bfloat16)


def mix_lanes(mix, dst):
    row, lane = iota((128, 1), 0), iota((1, 1280), 1)
    par, ml, r, k = row // 60, row % 60 // 12, row % 12 // 6, row % 6 // 3
    code = jnp.where(row < 120, ((r * 5 + ml) * 2 + par) * 2 + k, -1)
    kc = lane % 64
    seen = jnp.where(kc < 48, lane // 64 * 2 + kc // C, -2)
    same = code == seen
    wide = onehot(iota((C, 1280), 1) % 64 % C == iota((C, 1280), 0))
    for e in range(ENS):
        pick = onehot(iota((128, C), 1) == e * SHARE + iota((128, C), 0) % 3)
        tall = jnp.dot(pick, mix[...], preferred_element_type=F32).astype(BF)
        full = jnp.dot(tall, wide, preferred_element_type=F32)
        dst[e * 128 : (e + 1) * 128, :] = jnp.where(same, full, 0.0).astype(BF)


def scatter_lanes():
    e, row = np.meshgrid(np.arange(ENS), np.arange(128), indexing="ij")
    spot = row // 12 * 128 + row % 12 // 6 * 64 + row % 6 // 3 * C + e * SHARE + row % 3
    spot = np.where(row < 60, spot, -1).reshape(-1, 1)
    return (np.arange(640) == spot).astype(ml_dtypes.bfloat16)


def conv_half(weights, ext, prod, h):
    prod[...] = jnp.dot(weights[h], ext[...], preferred_element_type=F32)
    total = prod[0:72, 0:NLON]
    for q in range(1, 7):
        total = total + prod[q * 72 : (q + 1) * 72, q : q + NLON]
    return total


def soft_sign(gaps):
    return gaps * lax.rsqrt(gaps * gaps + 0.25)


class Exchange:
    def __init__(self, axis, count, me, block, slot, sent, landed, sems):
        self.axis, self.count, self.me = axis, count, me
        self.block, self.slot = block, slot
        self.sent, self.landed, self.sems = sent, landed, sems

    def device(self, peer):
        if self.axis is None:
            return {"ens": peer // BANDS, "lat": lax.rem(peer, BANDS)}
        return {self.axis: peer}

    def copy(self, source, target, peer):
        return pltpu.make_async_remote_copy(
            src_ref=source,
            dst_ref=target,
            send_sem=self.sems.at[0],
            recv_sem=self.sems.at[1],
            device_id=self.device(peer),
            device_id_type=MESH,
        )

    def start(self):
        def step(s, carry):
            peer = lax.rem(self.me + s, self.count)
            self.copy(self.block(peer), self.slot(self.me), peer).start()
            return carry

        lax.fori_loop(1, self.count, step, 0)

    def whole(self):
        return self.copy(self.sent, self.landed, lax.rem(self.me + 1, self.count))

    def arrived(self):
        self.whole().wait_recv()

    def done(self):
        self.whole().wait_send()


def kernel(
    x_hbm, leg_hbm, kern_hbm, table_hbm, mix_hbm, truth, order_hbm, gather_hbm, scatter_hbm,
    out, score,
    x, legl, table, kern, mix, order, window, wide, taps, placing, target, chosen,
    low, high, low2, high2, weights, flipped, wtmp, ext, prod, act, slope, hid,
    legf, legsend, legrecv, legall, leg,
    flat, stage, more, send1, recv1, coeff, grads, send4, recv4, send5, recv5,
    left, turn, regroup, mixing, regroup5,
    load_sems, halo_sems, halo2_sems, leg_sems, leg2_sems, sems1, sems4, sems5, entered,
):
    me = lax.axis_index("lat")
    em = lax.axis_index("ens")
    after = lax.rem(me + 1, BANDS)
    before = lax.rem(me + BANDS - 1, BANDS)

    m0 = me * ORDERS
    base = jnp.minimum(m0 // 8 * 8, M - 16)
    loads = [
        pltpu.make_async_copy(source, target_, load_sems.at[n])
        for n, (source, target_) in enumerate(
            [
                (leg_hbm, legl),
                (x_hbm, x),
                (truth.at[:, :, pl.ds(pl.multiple_of(base, 8), 16), :], window),
                (table_hbm, table),
                (kern_hbm, kern),
                (mix_hbm, mix),
                (order_hbm, order),
                (gather_hbm, regroup),
                (scatter_hbm, regroup5),
            ]
        )
    ]
    for load in loads:
        load.start()
    barrier = pltpu.get_barrier_semaphore()

    def greet(axis, count, mine):
        def step(s, carry):
            pl.semaphore_signal(
                barrier, 1, device_id={axis: lax.rem(mine + s, count)}, device_id_type=MESH
            )
            return carry

        lax.fori_loop(1, count, step, 0)

    greet("lat", BANDS, me)
    greet("ens", ENS, em)
    pl.semaphore_wait(barrier, BANDS - 1 + ENS - 1)

    def tell(s, carry):
        pl.semaphore_signal(
            entered, 1, device_id={"ens": lax.rem(em + s, ENS)}, device_id_type=MESH
        )
        return carry

    lax.fori_loop(1, ENS, tell, 0)

    def halo(source, lo, hi, sems, k):
        return (
            pltpu.make_async_remote_copy(
                src_ref=source.at[k, 1], dst_ref=lo.at[k],
                send_sem=sems.at[0, k], recv_sem=sems.at[1, k],
                device_id={"lat": after}, device_id_type=MESH,
            ),
            pltpu.make_async_remote_copy(
                src_ref=source.at[k, 0], dst_ref=hi.at[k],
                send_sem=sems.at[2, k], recv_sem=sems.at[3, k],
                device_id={"lat": before}, device_id_type=MESH,
            ),
        )

    halos = [halo(x_hbm, low, high, halo_sems, k) for k in range(2)]
    for pair in halos:
        for copy in pair:
            copy.start()

    loads[0].wait()
    for i in range(ROWS):
        legf[0, i] = legl[i, :, 0:128].astype(F32)
        legf[1, i] = jnp.concatenate(
            [legl[i, :, 128:L].astype(F32), jnp.zeros((M, 256 - L), F32)], axis=1
        )
    for q in range(4):
        n = jnp.minimum(em * 4 + q, 29)
        for b in range(2):
            stage[:, q * 2 + b, :] = legf[
                b, n // ORDERS, pl.ds(lax.rem(n, ORDERS), BANDS, stride=ORDERS), :
            ]
    legsend[...] = stage[...].astype(BF)
    legx = Exchange(
        "lat", BANDS, me, lambda p: legsend.at[p], lambda m: legrecv.at[m],
        legsend.at[pl.ds(0, BANDS - 1)], legrecv.at[pl.ds(0, BANDS - 1)], leg_sems,
    )
    legx.start()
    legrecv[me] = legsend[me]
    loads[4].wait()
    tile_taps(kern, taps)
    spread_weights(taps, weights, wtmp, False)
    loads[5].wait()
    place_mix(mix, placing)

    def fill_halo(lo, hi, k, h):
        if h == 0:
            edge = wrapped(lo[k].astype(F32))
            ext[144:216, :] = jnp.where(me > 0, edge, 0.0).astype(BF)
        else:
            edge = wrapped(hi[k].astype(F32))
            ext[144:216, :] = jnp.where(me < BANDS - 1, edge, 0.0).astype(BF)

    loads[1].wait()
    loads[3].wait()
    c0 = math.sqrt(2.0 / math.pi)
    spec = jnp.zeros((2 * M, 384), F32)
    for k in range(2):
        ext[0:72, :] = wrapped(x[k, 0])
        ext[72:144, :] = wrapped(x[k, 1])
        for h in range(2):
            halos[k][h].wait_recv()
            fill_halo(low, high, k, h)
            v = x[k, h].astype(F32) + conv_half(weights, ext, prod, h)
            sq = v * v
            t = jnp.tanh(c0 * v * (1.0 + 0.044715 * sq))
            half = 0.5 * (1.0 + t)
            act[h * 72 : (h + 1) * 72, :] = (v * half).astype(BF)
            slope[k, h] = (half + 0.5 * v * (1.0 - t * t) * (c0 * (1.0 + 0.134145 * sq))).astype(BF)
        waves = lax.dot_general(
            table[...], act[...], (((1,), (1,)), ((), ())), preferred_element_type=F32
        ).astype(BF)
        spec = spec + jnp.dot(waves, placing[k], preferred_element_type=F32)
        if k == 0:
            legx.arrived()
            legx2 = Exchange(
                "ens", ENS, em, lambda p: legrecv, lambda m: legall.at[m],
                legall.at[pl.ds(0, ENS - 1)], legall.at[pl.ds(0, ENS - 1)], leg2_sems,
            )
            legx2.start()
            legall[em] = legrecv[...]
    spec = spec.astype(BF)
    lined = jnp.concatenate(
        [
            jnp.concatenate(
                [spec[a * 32 : (a + 1) * 32, t * 128 : (t + 1) * 128] for a in range(10)], axis=1
            )
            for t in range(3)
        ],
        axis=0,
    )
    loads[7].wait()
    lined = jnp.dot(lined, regroup[...], preferred_element_type=F32)

    def tile(e, t):
        return pl.ds(e * 128 + t, BANDS, stride=4)

    for e in range(ENS):
        for t in range(3):
            flat[tile(e, t), :] = lined[t * 32 : (t + 1) * 32, e * 128 : (e + 1) * 128]
        flat[tile(e, 3), :] = jnp.zeros((BANDS, 128), F32)
    send1[...] = flat[...].reshape(WORLD, 4, 128).astype(BF)
    self_at = em * BANDS + me

    def swap_all(send, recv, sems):
        exchange = Exchange(
            None, WORLD, self_at, lambda p: send.at[p], lambda m: recv.at[m],
            send.at[pl.ds(0, WORLD - 1)], recv.at[pl.ds(0, WORLD - 1)], sems,
        )
        return exchange

    pl.semaphore_wait(entered, ENS - 1)
    x1 = swap_all(send1, recv1, sems1)
    x1.start()
    recv1[self_at] = send1[self_at]

    loads[2].wait()
    wide[0] = window[:, :, :, 0:128].astype(F32).reshape(2 * C, 16, 128)
    wide[1] = jnp.concatenate(
        [
            window[:, :, :, 128:L].astype(F32).reshape(2 * C, 16, L - 128),
            jnp.zeros((2 * C, 16, 256 - L), F32),
        ],
        axis=2,
    )
    lane = iota((80, 128), 1)

    def folded(v):
        return jnp.where(
            lane % 64 < 60, jnp.where(lane < 64, v[0:80], pltpu.roll(v[80:160], 64, 1)), 0.0
        )

    cr, at = iota((2 * C, 128), 0), iota((2 * C, 128), 1)
    mine = (cr // 2 == em * SHARE + at % 3) & (cr % 2 == at % 12 // 6)
    goal0, goal1 = jnp.zeros((128, 128), F32), jnp.zeros((128, 128), F32)
    for ml in range(ORDERS):
        spot = onehot(mine & (at // 12 == ml))
        for b in range(2):
            part = wide[b, :, m0 - base + ml, :].astype(BF)
            t = lax.dot_general(part, spot, (((0,), (0,)), ((), ())), preferred_element_type=F32)
            if b == 0:
                goal0 = goal0 + t
            else:
                goal1 = goal1 + t
    target[...] = folded(jnp.concatenate([goal0, goal1[0 : L - 128]], axis=0))
    place = iota((L, L), 0)
    spots = onehot(iota((L, L), 1) == place % BANDS * 5 + place // BANDS)
    loads[6].wait()
    kept = onehot(place == jnp.broadcast_to(order[...], (L, L)))
    chosen[...] = lax.dot_general(
        spots, kept, (((1,), (1,)), ((), ())), preferred_element_type=F32
    ).astype(BF)

    legx2.arrived()
    more[...] = legall[...].astype(F32)
    for ml in range(ORDERS):
        for i in range(ROWS):
            n, j = i * ORDERS + ml, (i % 2) * 3 + i // 2
            at = slice(j * 32, (j + 1) * 32)
            leg[ml, at, 0:128] = more[n // 4, :, n % 4 * 2, :].astype(BF)
            leg[ml, at, 128:L] = more[n // 4, :, n % 4 * 2 + 1, 0 : L - 128].astype(BF)
    mix_lanes(mix, mixing)

    x1.arrived()

    def arranged(recv):
        flat[...] = recv[...].astype(F32).reshape(WORLD * 4, 128)
        return jnp.concatenate(
            [
                jnp.concatenate([flat[tile(e, t), :] for e in range(ENS)], axis=1)
                for t in range(3)
            ],
            axis=0,
        )

    waves = arranged(recv1)
    kind = iota((96, 1024), 1) % 128 // 12
    acc = jnp.zeros((L, 1024), F32)
    for ml in range(ORDERS):
        both = jnp.concatenate(
            [jnp.where(kind == ml, waves, 0.0), jnp.where(kind == ml + 5, waves, 0.0)], axis=0
        ).astype(BF)
        acc = acc + lax.dot_general(
            leg[ml], both, (((0,), (0,)), ((), ())), preferred_element_type=F32
        )
    for e in range(ENS):
        v = acc[:, e * 128 : (e + 1) * 128]
        coeff[e] = folded(v + pltpu.roll(v, 68, 1))

    small = iota((16, 128), 1) % 64

    def other(v):
        return jnp.where(small % 6 < 3, pltpu.roll(v, 125, 1), pltpu.roll(v, 3, 1))

    def step(s, carry):
        at = pl.ds(pl.multiple_of(s * 16, 16), 16)
        u = [coeff[a, at, :] for a in range(ENS)]
        w = [jnp.where(small < 60, other(v), 0.0) for v in u]
        goal = target[at, :]
        plus = [jnp.zeros((16, 128), F32)] * ENS
        for b in range(ENS):
            turned = jnp.zeros((16, 128), F32)
            for a in range(b):
                one = soft_sign(u[a] - u[b])
                two = soft_sign(u[a] - w[b])
                plus[a] = plus[a] + (one + two)
                plus[b] = plus[b] - one
                turned = turned + two
            plus[b] = plus[b] + soft_sign(u[b] - w[b])
            plus[b] = plus[b] - jnp.where(small < 60, other(turned), 0.0)
        for a in range(ENS):
            coeff[a, at, :] = soft_sign(u[a] - goal) / 16.0 - plus[a] / 240.0
        return carry

    lax.fori_loop(0, 5, step, 0)
    for e in range(ENS):
        g = coeff[e]
        tall = jnp.concatenate([g, pltpu.roll(g, 64, 1)], axis=0)
        grads[:, e * 128 : (e + 1) * 128] = jnp.where(iota((L, 128), 1) < 60, tall, 0.0).astype(BF)
    kind = iota((L, 1024), 1) % 128 // 12
    acc = jnp.zeros((192, 1024), F32)
    for ml in range(ORDERS):
        g = jnp.where(kind == ml, grads[...].astype(F32), 0.0).astype(BF)
        acc = acc + jnp.dot(leg[ml], g, preferred_element_type=F32)
    for e in range(ENS):
        for t in range(3):
            even = acc[t * 32 : (t + 1) * 32, e * 128 : (e + 1) * 128]
            odd = acc[96 + t * 32 : 96 + (t + 1) * 32, e * 128 : (e + 1) * 128]
            flat[tile(e, t), :] = even + pltpu.roll(odd, 60, 1)
    send4[...] = flat[...].reshape(WORLD, 4, 128).astype(BF)
    x4 = swap_all(send4, recv4, sems4)
    x4.start()
    recv4[self_at] = send4[self_at]
    o = jnp.dot(chosen[...], grads[...], preferred_element_type=F32)
    for e in range(ENS):
        part = [o[j * 32 : (j + 1) * 32, e * 128 : (e + 1) * 128] for j in range(5)]
        for t in range(2):
            flat[tile(e, t), :] = part[2 * t] + pltpu.roll(part[2 * t + 1], 64, 1)
        flat[tile(e, 2), :] = part[4]
    send5[...] = flat[...].reshape(WORLD, 4, 128).astype(BF)
    x5 = swap_all(send5, recv5, sems5)
    recv5[self_at] = send5[self_at]

    spread_weights(taps, flipped, wtmp, True)
    x4.arrived()
    x5.start()
    lined = jnp.dot(arranged(recv4).astype(BF), mixing[...], preferred_element_type=F32)
    for t in range(3):
        for r in range(2):
            q = jnp.concatenate(
                [
                    lined[t * 32 : (t + 1) * 32, (r * 5 + ml) * 128 : (r * 5 + ml + 1) * 128]
                    for ml in range(ORDERS)
                ],
                axis=0,
            )
            qt = q.T
            for par in range(2):
                for k in range(2):
                    at = par * 64 + k * C
                    i = 2 * t + par
                    left[r, k, i * C : (i + 1) * C, :] = qt[at : at + C, :]
    halos2 = []
    for k in range(2):
        grad = jnp.dot(left[0, k].astype(BF), table[0:M, :], preferred_element_type=F32)
        grad = grad + jnp.dot(left[1, k].astype(BF), table[M:, :], preferred_element_type=F32)
        for h in range(2):
            hid[k, h] = (grad[h * 72 : (h + 1) * 72] * slope[k, h].astype(F32)).astype(BF)
        pair = halo(hid, low2, high2, halo2_sems, k)
        for copy in pair:
            copy.start()
        halos2.append(pair)

    for k in range(2):
        ext[0:72, :] = wrapped(hid[k, 0])
        ext[72:144, :] = wrapped(hid[k, 1])
        for h in range(2):
            halos2[k][h].wait_recv()
            fill_halo(low2, high2, k, h)
            out[k, h] = (hid[k, h].astype(F32) + conv_half(flipped, ext, prod, h)).astype(BF)
        if k == 0:
            x5.arrived()
            got = arranged(recv5)
            lined = []
            for j in range(5):
                v = got[j // 2 * 32 : j // 2 * 32 + 32]
                if j % 2:
                    v = jnp.concatenate(
                        [pltpu.roll(v[:, e * 128 : (e + 1) * 128], 64, 1) for e in range(ENS)], axis=1
                    )
                lined.append(v)
            lined = jnp.concatenate(lined, axis=0).astype(BF)
            loads[8].wait()
            lined = jnp.dot(lined, regroup5[...], preferred_element_type=F32)
            for j in range(5):
                for ml in range(ORDERS):
                    turn[pl.ds(ml, BANDS, stride=ORDERS), :] = lined[
                        j * 32 : (j + 1) * 32, ml * 128 : (ml + 1) * 128
                    ]
                qt = turn[...].T
                for r in range(2):
                    for k in range(2):
                        score[k, :, j, r, :] = qt[r * 64 + k * 24 : r * 64 + k * 24 + 24, :]

    for pairs in (halos, halos2):
        for pair in pairs:
            for copy in pair:
                copy.wait_send()
    for exchange in (legx, legx2, x1, x4, x5):
        exchange.done()


HALF = (2, 2, 72, NLON)
CHUNK = (WORLD, 4, 128)


def whole(*args):
    vmem = pl.BlockSpec(memory_space=pltpu.VMEM)
    far = pl.BlockSpec(memory_space=pltpu.HBM)
    pair = pltpu.SemaphoreType.DMA((2,))
    halo = (2, 72, NLON)
    eighth = (BANDS, 8, 128)
    scratch = [
        (HALF, BF), ((ROWS, M, L), BF), ((2 * M, NLON), BF), ((7, 7, C), F32), ((C, C), BF),
        ((1, L), jnp.int32), ((C, 2, 16, L), BF),
        ((2, 2 * C, 16, 128), F32), ((7, 7, 216), F32), ((2, 144, 384), BF), ((80, 128), F32),
        ((L, L), BF),
        (halo, BF), (halo, BF), (halo, BF), (halo, BF),
        ((2, 504, 216), BF), ((2, 504, 216), BF), ((504, 216), F32),
        ((216, 1536), BF), ((504, 1536), F32), ((144, NLON), BF), (HALF, BF), (HALF, BF),
        ((2, ROWS, M, 128), F32), (eighth, BF), (eighth, BF), ((ENS,) + eighth, BF),
        ((ORDERS, 192, L), BF),
        ((WORLD * 4, 128), F32), (eighth, F32), ((ENS,) + eighth, F32), (CHUNK, BF), (CHUNK, BF),
        ((ENS, 80, 128), F32), ((L, 1024), BF), (CHUNK, BF), (CHUNK, BF), (CHUNK, BF), (CHUNK, BF),
        ((2, 2, 144, M), F32), ((M, 128), F32),
        ((1280, 1024), BF), ((1024, 1280), BF), ((1024, 640), BF),
    ]
    return pl.pallas_call(
        kernel,
        out_shape=[
            jax.ShapeDtypeStruct(HALF, BF),
            jax.ShapeDtypeStruct((2, C, 5, 2, M), F32),
        ],
        in_specs=[far] * len(args),
        out_specs=[vmem, vmem],
        scratch_shapes=[pltpu.VMEM(s, d) for s, d in scratch]
        + [pltpu.SemaphoreType.DMA((9,))]
        + [pltpu.SemaphoreType.DMA((4, 2))] * 2
        + [pair] * 5
        + [pltpu.SemaphoreType.REGULAR],
        compiler_params=pltpu.CompilerParams(
            vmem_limit_bytes=62 << 20, collective_id=0, has_side_effects=True
        ),
    )(*args)


def local(fields, depth_kernel, mix_weight, legendre, truth, degree_order):
    table = jnp.asarray(wave_table())
    x = jnp.transpose(fields, (0, 2, 1, 3)).reshape(HALF)
    kern = jnp.transpose(depth_kernel, (1, 2, 0))
    out, score = whole(
        x, legendre, kern, table, mix_weight, truth, degree_order.reshape(1, L),
        jnp.asarray(gather_lanes()), jnp.asarray(scatter_lanes()),
    )
    grad_fields = jnp.transpose(out.reshape(2, ROWS, C, NLON), (0, 2, 1, 3))
    return grad_fields, jnp.transpose(score, (0, 1, 3, 4, 2))


def solution(mesh):
    placed = (P("ens", None, "lat", None), P(), P(), P("lat", None, None), P(), P())
    return jax.shard_map(
        local,
        mesh=mesh,
        in_specs=placed,
        out_specs=(P("ens", None, "lat", None), P("ens", None, None, None, "lat")),
        check_vma=False,
    )
```

```python
import math

import jax
import jax.numpy as jnp
import ml_dtypes
import numpy as np
from jax import lax
from jax.experimental import pallas as pl
from jax.experimental.pallas import tpu as pltpu
from jax.sharding import PartitionSpec as P

C = 24
NLON = 1440
M = 160
L = 160
BANDS = 32
ROWS = 6
ORDERS = M // BANDS
ENS = 8
WORLD = ENS * BANDS
SHARE = C // ENS
BF = jnp.bfloat16
F32 = jnp.float32
MESH = pl.DeviceIdType.MESH


def wave_table():
    m = (np.arange(BANDS)[None, :] * ORDERS + np.arange(ORDERS)[:, None]).reshape(-1)
    angles = (m[:, None] * np.arange(NLON)[None, :] % NLON) * (2.0 * math.pi / NLON)
    both = np.concatenate([np.cos(angles), -np.sin(angles)], axis=0) / math.sqrt(NLON)
    return both.astype(np.float32).astype(ml_dtypes.bfloat16)


def wrapped(x):
    return jnp.concatenate([x[:, NLON - 3 :], x, x[:, :93]], axis=1)


def iota(shape, axis):
    return lax.broadcasted_iota(jnp.int32, shape, axis)


def onehot(hit):
    return jnp.where(hit, 1.0, 0.0).astype(BF)


def tile_taps(kern, taps):
    again = onehot(iota((C, 216), 1) % C == iota((C, 216), 0))
    for p in range(7):
        taps[p] = jnp.dot(kern[p].astype(BF), again, preferred_element_type=F32)


def spread_weights(taps, dst, tmp, flip):
    lane = iota((C, 216), 1)
    same = lane % C == iota((C, 216), 0)
    for h in range(2):
        row = lane // C
        window = lax.rem(row + 3, 9) if h == 0 else row
        masks = [same & (window == g) for g in range(9)]
        for q in range(7):
            tap = []
            for p in range(7):
                a, b = (6 - p, 6 - q) if flip else (p, q)
                tap.append(jnp.broadcast_to(taps[a, b : b + 1, :], (C, 216)))
            for i in range(3):
                total = jnp.zeros((C, 216), F32)
                for p in range(7):
                    total = jnp.where(masks[i + p], tap[p], total)
                tmp[q * 72 + i * 24 : q * 72 + i * 24 + 24, :] = total
        dst[h] = tmp[...].astype(BF)


def place_mix(mix, placing):
    row = iota((144, C), 0)
    tall = lax.dot_general(
        onehot(row % C == iota((144, C), 1)), mix[...], (((1,), (1,)), ((), ())),
        preferred_element_type=F32,
    ).astype(BF)
    lane = iota((C, 384), 1)
    q = lane % 16
    channel = lane % 128 // 16 * SHARE + q % 3
    full_lane = iota((144, 384), 1)
    line = full_lane // 128 * 2 + full_lane % 16 // 6
    same = (iota((144, 384), 0) // C == line) & (full_lane % 16 < 12)
    for k in range(2):
        wide = onehot((channel == iota((C, 384), 0)) & (q % 6 // 3 == k))
        full = jnp.dot(tall, wide, preferred_element_type=F32)
        placing[k] = jnp.where(same, full, 0.0).astype(BF)


def gather_lanes():
    a, e, q = np.meshgrid(np.arange(10), np.arange(ENS), np.arange(16), indexing="ij")
    spot = e * 128 + q // 6 * 60 + a % ORDERS * 12 + a // ORDERS * 6 + q % 6
    spot = np.where(q < 12, spot, -1).reshape(-1, 1)
    return (np.arange(1024) == spot).astype(ml_dtypes.bfloat16)


def mix_lanes(mix, dst):
    row, lane = iota((128, 1), 0), iota((1, 1280), 1)
    par, ml, r, k = row // 60, row % 60 // 12, row % 12 // 6, row % 6 // 3
    code = jnp.where(row < 120, ((r * 5 + ml) * 2 + par) * 2 + k, -1)
    kc = lane % 64
    seen = jnp.where(kc < 48, lane // 64 * 2 + kc // C, -2)
    same = code == seen
    wide = onehot(iota((C, 1280), 1) % 64 % C == iota((C, 1280), 0))
    for e in range(ENS):
        pick = onehot(iota((128, C), 1) == e * SHARE + iota((128, C), 0) % 3)
        tall = jnp.dot(pick, mix[...], preferred_element_type=F32).astype(BF)
        full = jnp.dot(tall, wide, preferred_element_type=F32)
        dst[e * 128 : (e + 1) * 128, :] = jnp.where(same, full, 0.0).astype(BF)


def scatter_lanes():
    e, row = np.meshgrid(np.arange(ENS), np.arange(128), indexing="ij")
    spot = row // 12 * 128 + row % 12 // 6 * 64 + row % 6 // 3 * C + e * SHARE + row % 3
    spot = np.where(row < 60, spot, -1).reshape(-1, 1)
    return (np.arange(640) == spot).astype(ml_dtypes.bfloat16)


def conv_half(weights, ext, prod, h):
    prod[...] = jnp.dot(weights[h], ext[...], preferred_element_type=F32)
    total = prod[0:72, 0:NLON]
    for q in range(1, 7):
        total = total + prod[q * 72 : (q + 1) * 72, q : q + NLON]
    return total


def soft_sign(gaps):
    return gaps * lax.rsqrt(gaps * gaps + 0.25)


class Exchange:
    def __init__(self, axis, count, me, block, slot, sent, landed, sems):
        self.axis, self.count, self.me = axis, count, me
        self.block, self.slot = block, slot
        self.sent, self.landed, self.sems = sent, landed, sems

    def copy(self, source, target, device):
        return pltpu.make_async_remote_copy(
            src_ref=source,
            dst_ref=target,
            send_sem=self.sems.at[0],
            recv_sem=self.sems.at[1],
            device_id=device,
            device_id_type=MESH,
        )

    def start(self):
        def step(s, carry):
            peer = lax.rem(self.me + s, self.count)
            self.copy(self.block(peer), self.slot(self.me), {self.axis: peer}).start()
            return carry

        lax.fori_loop(1, self.count, step, 0)

    def whole(self):
        return self.copy(self.sent, self.landed, {self.axis: lax.rem(self.me + 1, self.count)})

    def arrived(self):
        self.whole().wait_recv()

    def done(self):
        self.whole().wait_send()


class Everyone(Exchange):
    def __init__(self, send, recv, em, me, sems):
        self.send, self.recv, self.em, self.lat, self.sems = send, recv, em, me, sems
        self.at = em * BANDS + me

    def start(self):
        owners = [lax.rem(self.em + u, ENS) for u in range(ENS)]

        def one(e, band):
            self.copy(
                self.send.at[e * BANDS + band], self.recv.at[self.at], {"ens": e, "lat": band}
            ).start()

        def step(s, carry):
            band = lax.rem(self.lat + s, BANDS)
            for e in owners:
                one(e, band)
            return carry

        lax.fori_loop(1, BANDS, step, 0)
        for e in owners[1:]:
            one(e, self.lat)

    def whole(self):
        rest = pl.ds(0, WORLD - 1)
        return self.copy(
            self.send.at[rest], self.recv.at[rest], {"lat": lax.rem(self.lat + 1, BANDS)}
        )


def kernel(
    x_hbm, leg_hbm, kern_hbm, table_hbm, mix_hbm, truth, order_hbm, gather_hbm, scatter_hbm,
    out, score,
    x, legl, table, kern, mix, order, window, wide, taps, placing, target, chosen,
    low, high, low2, high2, weights, flipped, wtmp, ext, prod, act, slope, hid,
    legf, legsend, legrecv, legall, leg,
    flat, stage, more, send1, recv1, coeff, grads, send4, recv4, send5, recv5,
    left, turn, regroup, mixing, regroup5,
    load_sems, halo_sems, halo2_sems, leg_sems, leg2_sems, sems1, sems4, sems5, entered,
):
    me = lax.axis_index("lat")
    em = lax.axis_index("ens")
    after = lax.rem(me + 1, BANDS)
    before = lax.rem(me + BANDS - 1, BANDS)

    m0 = me * ORDERS
    base = jnp.minimum(m0 // 8 * 8, M - 16)
    loads = [
        pltpu.make_async_copy(source, target_, load_sems.at[n])
        for n, (source, target_) in enumerate(
            [
                (leg_hbm, legl),
                (x_hbm, x),
                (truth.at[:, :, pl.ds(pl.multiple_of(base, 8), 16), :], window),
                (table_hbm, table),
                (kern_hbm, kern),
                (mix_hbm, mix),
                (order_hbm, order),
                (gather_hbm, regroup),
                (scatter_hbm, regroup5),
            ]
        )
    ]
    for load in loads:
        load.start()
    barrier = pltpu.get_barrier_semaphore()

    def greet(axis, count, mine):
        def step(s, carry):
            pl.semaphore_signal(
                barrier, 1, device_id={axis: lax.rem(mine + s, count)}, device_id_type=MESH
            )
            return carry

        lax.fori_loop(1, count, step, 0)

    greet("lat", BANDS, me)
    greet("ens", ENS, em)
    pl.semaphore_wait(barrier, BANDS - 1 + ENS - 1)

    def tell(s, carry):
        pl.semaphore_signal(
            entered, 1, device_id={"ens": lax.rem(em + s, ENS)}, device_id_type=MESH
        )
        return carry

    lax.fori_loop(1, ENS, tell, 0)

    def halo(source, lo, hi, sems, k):
        return (
            pltpu.make_async_remote_copy(
                src_ref=source.at[k, 1], dst_ref=lo.at[k],
                send_sem=sems.at[0, k], recv_sem=sems.at[1, k],
                device_id={"lat": after}, device_id_type=MESH,
            ),
            pltpu.make_async_remote_copy(
                src_ref=source.at[k, 0], dst_ref=hi.at[k],
                send_sem=sems.at[2, k], recv_sem=sems.at[3, k],
                device_id={"lat": before}, device_id_type=MESH,
            ),
        )

    halos = [halo(x_hbm, low, high, halo_sems, k) for k in range(2)]
    for pair in halos:
        for copy in pair:
            copy.start()

    loads[0].wait()
    for i in range(ROWS):
        legf[0, i] = legl[i, :, 0:128].astype(F32)
        legf[1, i] = jnp.concatenate(
            [legl[i, :, 128:L].astype(F32), jnp.zeros((M, 256 - L), F32)], axis=1
        )
    for q in range(4):
        n = jnp.minimum(em * 4 + q, 29)
        for b in range(2):
            stage[:, q * 2 + b, :] = legf[
                b, n // ORDERS, pl.ds(lax.rem(n, ORDERS), BANDS, stride=ORDERS), :
            ]
    legsend[...] = stage[...].astype(BF)
    legx = Exchange(
        "lat", BANDS, me, lambda p: legsend.at[p], lambda m: legrecv.at[m],
        legsend.at[pl.ds(0, BANDS - 1)], legrecv.at[pl.ds(0, BANDS - 1)], leg_sems,
    )
    legx.start()
    legrecv[me] = legsend[me]
    loads[4].wait()
    tile_taps(kern, taps)
    spread_weights(taps, weights, wtmp, False)
    loads[5].wait()
    place_mix(mix, placing)

    def fill_halo(lo, hi, k, h):
        if h == 0:
            edge = wrapped(lo[k].astype(F32))
            ext[144:216, :] = jnp.where(me > 0, edge, 0.0).astype(BF)
        else:
            edge = wrapped(hi[k].astype(F32))
            ext[144:216, :] = jnp.where(me < BANDS - 1, edge, 0.0).astype(BF)

    loads[1].wait()
    loads[3].wait()
    c0 = math.sqrt(2.0 / math.pi)
    spec = jnp.zeros((2 * M, 384), F32)
    for k in range(2):
        ext[0:72, :] = wrapped(x[k, 0])
        ext[72:144, :] = wrapped(x[k, 1])
        for h in range(2):
            halos[k][h].wait_recv()
            fill_halo(low, high, k, h)
            v = x[k, h].astype(F32) + conv_half(weights, ext, prod, h)
            sq = v * v
            t = jnp.tanh(c0 * v * (1.0 + 0.044715 * sq))
            half = 0.5 * (1.0 + t)
            act[h * 72 : (h + 1) * 72, :] = (v * half).astype(BF)
            slope[k, h] = (half + 0.5 * v * (1.0 - t * t) * (c0 * (1.0 + 0.134145 * sq))).astype(BF)
        waves = lax.dot_general(
            table[...], act[...], (((1,), (1,)), ((), ())), preferred_element_type=F32
        ).astype(BF)
        spec = spec + jnp.dot(waves, placing[k], preferred_element_type=F32)
        if k == 0:
            legx.arrived()
            legx2 = Exchange(
                "ens", ENS, em, lambda p: legrecv, lambda m: legall.at[m],
                legall.at[pl.ds(0, ENS - 1)], legall.at[pl.ds(0, ENS - 1)], leg2_sems,
            )
            legx2.start()
            legall[em] = legrecv[...]
    spec = spec.astype(BF)
    lined = jnp.concatenate(
        [
            jnp.concatenate(
                [spec[a * 32 : (a + 1) * 32, t * 128 : (t + 1) * 128] for a in range(10)], axis=1
            )
            for t in range(3)
        ],
        axis=0,
    )
    loads[7].wait()
    lined = jnp.dot(lined, regroup[...], preferred_element_type=F32)

    def tile(e, t):
        return pl.ds(e * 128 + t, BANDS, stride=4)

    for e in range(ENS):
        for t in range(3):
            flat[tile(e, t), :] = lined[t * 32 : (t + 1) * 32, e * 128 : (e + 1) * 128]
        flat[tile(e, 3), :] = jnp.zeros((BANDS, 128), F32)
    send1[...] = flat[...].reshape(WORLD, 4, 128).astype(BF)
    self_at = em * BANDS + me

    pl.semaphore_wait(entered, ENS - 1)
    x1 = Everyone(send1, recv1, em, me, sems1)
    x1.start()
    recv1[self_at] = send1[self_at]

    loads[2].wait()
    wide[0] = window[:, :, :, 0:128].astype(F32).reshape(2 * C, 16, 128)
    wide[1] = jnp.concatenate(
        [
            window[:, :, :, 128:L].astype(F32).reshape(2 * C, 16, L - 128),
            jnp.zeros((2 * C, 16, 256 - L), F32),
        ],
        axis=2,
    )
    lane = iota((80, 128), 1)

    def folded(v):
        return jnp.where(
            lane % 64 < 60, jnp.where(lane < 64, v[0:80], pltpu.roll(v[80:160], 64, 1)), 0.0
        )

    cr, at = iota((2 * C, 128), 0), iota((2 * C, 128), 1)
    mine = (cr // 2 == em * SHARE + at % 3) & (cr % 2 == at % 12 // 6)
    goal0, goal1 = jnp.zeros((128, 128), F32), jnp.zeros((128, 128), F32)
    for ml in range(ORDERS):
        spot = onehot(mine & (at // 12 == ml))
        for b in range(2):
            part = wide[b, :, m0 - base + ml, :].astype(BF)
            t = lax.dot_general(part, spot, (((0,), (0,)), ((), ())), preferred_element_type=F32)
            if b == 0:
                goal0 = goal0 + t
            else:
                goal1 = goal1 + t
    target[...] = folded(jnp.concatenate([goal0, goal1[0 : L - 128]], axis=0))
    place = iota((L, L), 0)
    spots = onehot(iota((L, L), 1) == place % BANDS * 5 + place // BANDS)
    loads[6].wait()
    kept = onehot(place == jnp.broadcast_to(order[...], (L, L)))
    chosen[...] = lax.dot_general(
        spots, kept, (((1,), (1,)), ((), ())), preferred_element_type=F32
    ).astype(BF)

    legx2.arrived()
    more[...] = legall[...].astype(F32)
    for ml in range(ORDERS):
        for i in range(ROWS):
            n, j = i * ORDERS + ml, (i % 2) * 3 + i // 2
            at = slice(j * 32, (j + 1) * 32)
            leg[ml, at, 0:128] = more[n // 4, :, n % 4 * 2, :].astype(BF)
            leg[ml, at, 128:L] = more[n // 4, :, n % 4 * 2 + 1, 0 : L - 128].astype(BF)
    mix_lanes(mix, mixing)

    x1.arrived()

    def arranged(recv):
        flat[...] = recv[...].astype(F32).reshape(WORLD * 4, 128)
        return jnp.concatenate(
            [
                jnp.concatenate([flat[tile(e, t), :] for e in range(ENS)], axis=1)
                for t in range(3)
            ],
            axis=0,
        )

    waves = arranged(recv1)
    kind = iota((96, 1024), 1) % 128 // 12
    acc = jnp.zeros((L, 1024), F32)
    for ml in range(ORDERS):
        both = jnp.concatenate(
            [jnp.where(kind == ml, waves, 0.0), jnp.where(kind == ml + 5, waves, 0.0)], axis=0
        ).astype(BF)
        acc = acc + lax.dot_general(
            leg[ml], both, (((0,), (0,)), ((), ())), preferred_element_type=F32
        )
    for e in range(ENS):
        v = acc[:, e * 128 : (e + 1) * 128]
        coeff[e] = folded(v + pltpu.roll(v, 68, 1))

    small = iota((16, 128), 1) % 64

    def other(v):
        return jnp.where(small % 6 < 3, pltpu.roll(v, 125, 1), pltpu.roll(v, 3, 1))

    def step(s, carry):
        at = pl.ds(pl.multiple_of(s * 16, 16), 16)
        u = [coeff[a, at, :] for a in range(ENS)]
        w = [jnp.where(small < 60, other(v), 0.0) for v in u]
        goal = target[at, :]
        plus = [jnp.zeros((16, 128), F32)] * ENS
        for b in range(ENS):
            turned = jnp.zeros((16, 128), F32)
            for a in range(b):
                one = soft_sign(u[a] - u[b])
                two = soft_sign(u[a] - w[b])
                plus[a] = plus[a] + (one + two)
                plus[b] = plus[b] - one
                turned = turned + two
            plus[b] = plus[b] + soft_sign(u[b] - w[b])
            plus[b] = plus[b] - jnp.where(small < 60, other(turned), 0.0)
        for a in range(ENS):
            coeff[a, at, :] = soft_sign(u[a] - goal) / 16.0 - plus[a] / 240.0
        return carry

    lax.fori_loop(0, 5, step, 0)
    for e in range(ENS):
        g = coeff[e]
        tall = jnp.concatenate([g, pltpu.roll(g, 64, 1)], axis=0)
        grads[:, e * 128 : (e + 1) * 128] = jnp.where(iota((L, 128), 1) < 60, tall, 0.0).astype(BF)
    kind = iota((L, 1024), 1) % 128 // 12
    acc = jnp.zeros((192, 1024), F32)
    for ml in range(ORDERS):
        g = jnp.where(kind == ml, grads[...].astype(F32), 0.0).astype(BF)
        acc = acc + jnp.dot(leg[ml], g, preferred_element_type=F32)
    for e in range(ENS):
        for t in range(3):
            even = acc[t * 32 : (t + 1) * 32, e * 128 : (e + 1) * 128]
            odd = acc[96 + t * 32 : 96 + (t + 1) * 32, e * 128 : (e + 1) * 128]
            flat[tile(e, t), :] = even + pltpu.roll(odd, 60, 1)
    send4[...] = flat[...].reshape(WORLD, 4, 128).astype(BF)
    x4 = Everyone(send4, recv4, em, me, sems4)
    x4.start()
    recv4[self_at] = send4[self_at]
    o = jnp.dot(chosen[...], grads[...], preferred_element_type=F32)
    for e in range(ENS):
        part = [o[j * 32 : (j + 1) * 32, e * 128 : (e + 1) * 128] for j in range(5)]
        for t in range(2):
            flat[tile(e, t), :] = part[2 * t] + pltpu.roll(part[2 * t + 1], 64, 1)
        flat[tile(e, 2), :] = part[4]
    send5[...] = flat[...].reshape(WORLD, 4, 128).astype(BF)
    x5 = Everyone(send5, recv5, em, me, sems5)
    recv5[self_at] = send5[self_at]

    spread_weights(taps, flipped, wtmp, True)
    x4.arrived()
    lined = jnp.dot(arranged(recv4).astype(BF), mixing[...], preferred_element_type=F32)
    for t in range(3):
        for r in range(2):
            q = jnp.concatenate(
                [
                    lined[t * 32 : (t + 1) * 32, (r * 5 + ml) * 128 : (r * 5 + ml + 1) * 128]
                    for ml in range(ORDERS)
                ],
                axis=0,
            )
            qt = q.T
            for par in range(2):
                for k in range(2):
                    at = par * 64 + k * C
                    i = 2 * t + par
                    left[r, k, i * C : (i + 1) * C, :] = qt[at : at + C, :]
    halos2 = []
    for k in range(2):
        grad = jnp.dot(left[0, k].astype(BF), table[0:M, :], preferred_element_type=F32)
        grad = grad + jnp.dot(left[1, k].astype(BF), table[M:, :], preferred_element_type=F32)
        for h in range(2):
            hid[k, h] = (grad[h * 72 : (h + 1) * 72] * slope[k, h].astype(F32)).astype(BF)
        pair = halo(hid, low2, high2, halo2_sems, k)
        for copy in pair:
            copy.start()
        halos2.append(pair)
    x5.start()

    for k in range(2):
        ext[0:72, :] = wrapped(hid[k, 0])
        ext[72:144, :] = wrapped(hid[k, 1])
        for h in range(2):
            halos2[k][h].wait_recv()
            fill_halo(low2, high2, k, h)
            out[k, h] = (hid[k, h].astype(F32) + conv_half(flipped, ext, prod, h)).astype(BF)
    x5.arrived()
    got = arranged(recv5)
    lined = []
    for j in range(5):
        v = got[j // 2 * 32 : j // 2 * 32 + 32]
        if j % 2:
            v = jnp.concatenate(
                [pltpu.roll(v[:, e * 128 : (e + 1) * 128], 64, 1) for e in range(ENS)], axis=1
            )
        lined.append(v)
    lined = jnp.concatenate(lined, axis=0).astype(BF)
    loads[8].wait()
    lined = jnp.dot(lined, regroup5[...], preferred_element_type=F32)
    for j in range(5):
        for ml in range(ORDERS):
            turn[pl.ds(ml, BANDS, stride=ORDERS), :] = lined[
                j * 32 : (j + 1) * 32, ml * 128 : (ml + 1) * 128
            ]
        qt = turn[...].T
        for r in range(2):
            for k in range(2):
                score[k, :, j, r, :] = qt[r * 64 + k * 24 : r * 64 + k * 24 + 24, :]

    for pairs in (halos, halos2):
        for pair in pairs:
            for copy in pair:
                copy.wait_send()
    for exchange in (legx, legx2, x1, x4, x5):
        exchange.done()


HALF = (2, 2, 72, NLON)
CHUNK = (WORLD, 4, 128)


def whole(*args):
    vmem = pl.BlockSpec(memory_space=pltpu.VMEM)
    far = pl.BlockSpec(memory_space=pltpu.HBM)
    pair = pltpu.SemaphoreType.DMA((2,))
    halo = (2, 72, NLON)
    eighth = (BANDS, 8, 128)
    scratch = [
        (HALF, BF), ((ROWS, M, L), BF), ((2 * M, NLON), BF), ((7, 7, C), F32), ((C, C), BF),
        ((1, L), jnp.int32), ((C, 2, 16, L), BF),
        ((2, 2 * C, 16, 128), F32), ((7, 7, 216), F32), ((2, 144, 384), BF), ((80, 128), F32),
        ((L, L), BF),
        (halo, BF), (halo, BF), (halo, BF), (halo, BF),
        ((2, 504, 216), BF), ((2, 504, 216), BF), ((504, 216), F32),
        ((216, 1536), BF), ((504, 1536), F32), ((144, NLON), BF), (HALF, BF), (HALF, BF),
        ((2, ROWS, M, 128), F32), (eighth, BF), (eighth, BF), ((ENS,) + eighth, BF),
        ((ORDERS, 192, L), BF),
        ((WORLD * 4, 128), F32), (eighth, F32), ((ENS,) + eighth, F32), (CHUNK, BF), (CHUNK, BF),
        ((ENS, 80, 128), F32), ((L, 1024), BF), (CHUNK, BF), (CHUNK, BF), (CHUNK, BF), (CHUNK, BF),
        ((2, 2, 144, M), F32), ((M, 128), F32),
        ((1280, 1024), BF), ((1024, 1280), BF), ((1024, 640), BF),
    ]
    return pl.pallas_call(
        kernel,
        out_shape=[
            jax.ShapeDtypeStruct(HALF, BF),
            jax.ShapeDtypeStruct((2, C, 5, 2, M), F32),
        ],
        in_specs=[far] * len(args),
        out_specs=[vmem, vmem],
        scratch_shapes=[pltpu.VMEM(s, d) for s, d in scratch]
        + [pltpu.SemaphoreType.DMA((9,))]
        + [pltpu.SemaphoreType.DMA((4, 2))] * 2
        + [pair] * 5
        + [pltpu.SemaphoreType.REGULAR],
        compiler_params=pltpu.CompilerParams(
            vmem_limit_bytes=62 << 20, collective_id=0, has_side_effects=True
        ),
    )(*args)


def local(fields, depth_kernel, mix_weight, legendre, truth, degree_order):
    table = jnp.asarray(wave_table())
    x = jnp.transpose(fields, (0, 2, 1, 3)).reshape(HALF)
    kern = jnp.transpose(depth_kernel, (1, 2, 0))
    out, score = whole(
        x, legendre, kern, table, mix_weight, truth, degree_order.reshape(1, L),
        jnp.asarray(gather_lanes()), jnp.asarray(scatter_lanes()),
    )
    grad_fields = jnp.transpose(out.reshape(2, ROWS, C, NLON), (0, 2, 1, 3))
    return grad_fields, jnp.transpose(score, (0, 1, 3, 4, 2))


def solution(mesh):
    placed = (P("ens", None, "lat", None), P(), P(), P("lat", None, None), P(), P())
    return jax.shard_map(
        local,
        mesh=mesh,
        in_specs=placed,
        out_specs=(P("ens", None, "lat", None), P("ens", None, None, None, "lat")),
        check_vma=False,
    )
```

```python
import math

import jax
import jax.numpy as jnp
import ml_dtypes
import numpy as np
from jax import lax
from jax.experimental import pallas as pl
from jax.experimental.pallas import tpu as pltpu
from jax.sharding import PartitionSpec as P

C = 24
NLON = 1440
M = 160
L = 160
BANDS = 32
ROWS = 6
ORDERS = M // BANDS
ENS = 8
WORLD = ENS * BANDS
SHARE = C // ENS
BF = jnp.bfloat16
F32 = jnp.float32
MESH = pl.DeviceIdType.MESH


def wave_table():
    m = (np.arange(BANDS)[None, :] * ORDERS + np.arange(ORDERS)[:, None]).reshape(-1)
    angles = (m[:, None] * np.arange(NLON)[None, :] % NLON) * (2.0 * math.pi / NLON)
    both = np.concatenate([np.cos(angles), -np.sin(angles)], axis=0) / math.sqrt(NLON)
    return both.astype(np.float32).astype(ml_dtypes.bfloat16)


def wrapped(x):
    return jnp.concatenate([x[:, NLON - 3 :], x, x[:, :93]], axis=1)


def iota(shape, axis):
    return lax.broadcasted_iota(jnp.int32, shape, axis)


def onehot(hit):
    return jnp.where(hit, 1.0, 0.0).astype(BF)


def tile_taps(kern, taps):
    again = onehot(iota((C, 216), 1) % C == iota((C, 216), 0))
    for p in range(7):
        taps[p] = jnp.dot(kern[p].astype(BF), again, preferred_element_type=F32)


def spread_weights(taps, dst, tmp, flip):
    lane = iota((C, 216), 1)
    same = lane % C == iota((C, 216), 0)
    for h in range(2):
        row = lane // C
        window = lax.rem(row + 3, 9) if h == 0 else row
        masks = [same & (window == g) for g in range(9)]
        for q in range(7):
            tap = []
            for p in range(7):
                a, b = (6 - p, 6 - q) if flip else (p, q)
                tap.append(jnp.broadcast_to(taps[a, b : b + 1, :], (C, 216)))
            for i in range(3):
                total = jnp.zeros((C, 216), F32)
                for p in range(7):
                    total = jnp.where(masks[i + p], tap[p], total)
                tmp[q * 72 + i * 24 : q * 72 + i * 24 + 24, :] = total
        dst[h] = tmp[...].astype(BF)


def place_mix(mix, placing):
    row = iota((144, C), 0)
    tall = lax.dot_general(
        onehot(row % C == iota((144, C), 1)), mix[...], (((1,), (1,)), ((), ())),
        preferred_element_type=F32,
    ).astype(BF)
    lane = iota((C, 384), 1)
    q = lane % 16
    channel = lane % 128 // 16 * SHARE + q % 3
    full_lane = iota((144, 384), 1)
    line = full_lane // 128 * 2 + full_lane % 16 // 6
    same = (iota((144, 384), 0) // C == line) & (full_lane % 16 < 12)
    for k in range(2):
        wide = onehot((channel == iota((C, 384), 0)) & (q % 6 // 3 == k))
        full = jnp.dot(tall, wide, preferred_element_type=F32)
        placing[k] = jnp.where(same, full, 0.0).astype(BF)


def gather_lanes():
    a, e, q = np.meshgrid(np.arange(10), np.arange(ENS), np.arange(16), indexing="ij")
    spot = e * 128 + q // 6 * 60 + a % ORDERS * 12 + a // ORDERS * 6 + q % 6
    spot = np.where(q < 12, spot, -1).reshape(-1, 1)
    return (np.arange(1024) == spot).astype(ml_dtypes.bfloat16)


def mix_lanes(mix, dst):
    row, lane = iota((128, 1), 0), iota((1, 1280), 1)
    par, ml, r, k = row // 60, row % 60 // 12, row % 12 // 6, row % 6 // 3
    code = jnp.where(row < 120, ((r * 5 + ml) * 2 + par) * 2 + k, -1)
    kc = lane % 64
    seen = jnp.where(kc < 48, lane // 64 * 2 + kc // C, -2)
    same = code == seen
    wide = onehot(iota((C, 1280), 1) % 64 % C == iota((C, 1280), 0))
    for e in range(ENS):
        pick = onehot(iota((128, C), 1) == e * SHARE + iota((128, C), 0) % 3)
        tall = jnp.dot(pick, mix[...], preferred_element_type=F32).astype(BF)
        full = jnp.dot(tall, wide, preferred_element_type=F32)
        dst[e * 128 : (e + 1) * 128, :] = jnp.where(same, full, 0.0).astype(BF)


def scatter_lanes():
    e, row = np.meshgrid(np.arange(ENS), np.arange(128), indexing="ij")
    spot = row // 12 * 128 + row % 12 // 6 * 64 + row % 6 // 3 * C + e * SHARE + row % 3
    spot = np.where(row < 60, spot, -1).reshape(-1, 1)
    return (np.arange(640) == spot).astype(ml_dtypes.bfloat16)


def conv_half(weights, ext, prod, h):
    prod[...] = jnp.dot(weights[h], ext[...], preferred_element_type=F32)
    total = prod[0:72, 0:NLON]
    for q in range(1, 7):
        total = total + prod[q * 72 : (q + 1) * 72, q : q + NLON]
    return total


def soft_sign(gaps):
    return gaps * lax.rsqrt(gaps * gaps + 0.25)


class Exchange:
    def __init__(self, axis, count, me, block, slot, sent, landed, sems):
        self.axis, self.count, self.me = axis, count, me
        self.block, self.slot = block, slot
        self.sent, self.landed, self.sems = sent, landed, sems

    def copy(self, source, target, device):
        return pltpu.make_async_remote_copy(
            src_ref=source,
            dst_ref=target,
            send_sem=self.sems.at[0],
            recv_sem=self.sems.at[1],
            device_id=device,
            device_id_type=MESH,
        )

    def start(self):
        def step(s, carry):
            peer = lax.rem(self.me + s, self.count)
            self.copy(self.block(peer), self.slot(self.me), {self.axis: peer}).start()
            return carry

        lax.fori_loop(1, self.count, step, 0)

    def whole(self):
        return self.copy(self.sent, self.landed, {self.axis: lax.rem(self.me + 1, self.count)})

    def arrived(self):
        self.whole().wait_recv()

    def done(self):
        self.whole().wait_send()


class Everyone(Exchange):
    def __init__(self, send, recv, em, me, sems):
        self.send, self.recv, self.em, self.lat, self.sems = send, recv, em, me, sems
        self.at = em * BANDS + me

    def start(self):
        owners = [lax.rem(self.em + u, ENS) for u in range(ENS)]

        def one(e, band):
            self.copy(
                self.send.at[e * BANDS + band], self.recv.at[self.at], {"ens": e, "lat": band}
            ).start()

        for u, e in enumerate(owners):

            def step(s, carry, e=e):
                one(e, lax.rem(self.lat + s, BANDS))
                return carry

            lax.fori_loop(0 if u else 1, BANDS, step, 0)

    def whole(self):
        rest = pl.ds(0, WORLD - 1)
        return self.copy(
            self.send.at[rest], self.recv.at[rest], {"lat": lax.rem(self.lat + 1, BANDS)}
        )


def kernel(
    x_hbm, leg_hbm, kern_hbm, table_hbm, mix_hbm, truth, order_hbm, gather_hbm, scatter_hbm,
    out, score,
    x, legl, table, kern, mix, order, window, wide, taps, placing, target, chosen,
    low, high, low2, high2, weights, flipped, wtmp, ext, prod, act, slope, hid,
    legf, legsend, legrecv, legall, leg,
    flat, stage, more, send1, recv1, coeff, grads, send4, recv4, send5, recv5,
    left, turn, regroup, mixing, regroup5,
    load_sems, halo_sems, halo2_sems, leg_sems, leg2_sems, sems1, sems4, sems5, entered,
):
    me = lax.axis_index("lat")
    em = lax.axis_index("ens")
    after = lax.rem(me + 1, BANDS)
    before = lax.rem(me + BANDS - 1, BANDS)

    m0 = me * ORDERS
    base = jnp.minimum(m0 // 8 * 8, M - 16)
    loads = [
        pltpu.make_async_copy(source, target_, load_sems.at[n])
        for n, (source, target_) in enumerate(
            [
                (leg_hbm, legl),
                (x_hbm, x),
                (truth.at[:, :, pl.ds(pl.multiple_of(base, 8), 16), :], window),
                (table_hbm, table),
                (kern_hbm, kern),
                (mix_hbm, mix),
                (order_hbm, order),
                (gather_hbm, regroup),
                (scatter_hbm, regroup5),
            ]
        )
    ]
    for load in loads:
        load.start()
    barrier = pltpu.get_barrier_semaphore()

    def greet(axis, count, mine):
        def step(s, carry):
            pl.semaphore_signal(
                barrier, 1, device_id={axis: lax.rem(mine + s, count)}, device_id_type=MESH
            )
            return carry

        lax.fori_loop(1, count, step, 0)

    greet("lat", BANDS, me)
    greet("ens", ENS, em)
    pl.semaphore_wait(barrier, BANDS - 1 + ENS - 1)

    def tell(s, carry):
        pl.semaphore_signal(
            entered, 1, device_id={"ens": lax.rem(em + s, ENS)}, device_id_type=MESH
        )
        return carry

    lax.fori_loop(1, ENS, tell, 0)

    def halo(source, lo, hi, sems, k):
        return (
            pltpu.make_async_remote_copy(
                src_ref=source.at[k, 1], dst_ref=lo.at[k],
                send_sem=sems.at[0, k], recv_sem=sems.at[1, k],
                device_id={"lat": after}, device_id_type=MESH,
            ),
            pltpu.make_async_remote_copy(
                src_ref=source.at[k, 0], dst_ref=hi.at[k],
                send_sem=sems.at[2, k], recv_sem=sems.at[3, k],
                device_id={"lat": before}, device_id_type=MESH,
            ),
        )

    halos = [halo(x_hbm, low, high, halo_sems, k) for k in range(2)]
    for pair in halos:
        for copy in pair:
            copy.start()

    loads[0].wait()
    for i in range(ROWS):
        legf[0, i] = legl[i, :, 0:128].astype(F32)
        legf[1, i] = jnp.concatenate(
            [legl[i, :, 128:L].astype(F32), jnp.zeros((M, 256 - L), F32)], axis=1
        )
    for q in range(4):
        n = jnp.minimum(em * 4 + q, 29)
        for b in range(2):
            stage[:, q * 2 + b, :] = legf[
                b, n // ORDERS, pl.ds(lax.rem(n, ORDERS), BANDS, stride=ORDERS), :
            ]
    legsend[...] = stage[...].astype(BF)
    legx = Exchange(
        "lat", BANDS, me, lambda p: legsend.at[p], lambda m: legrecv.at[m],
        legsend.at[pl.ds(0, BANDS - 1)], legrecv.at[pl.ds(0, BANDS - 1)], leg_sems,
    )
    legx.start()
    legrecv[me] = legsend[me]
    loads[4].wait()
    tile_taps(kern, taps)
    spread_weights(taps, weights, wtmp, False)
    loads[5].wait()
    place_mix(mix, placing)

    def fill_halo(lo, hi, k, h):
        if h == 0:
            edge = wrapped(lo[k].astype(F32))
            ext[144:216, :] = jnp.where(me > 0, edge, 0.0).astype(BF)
        else:
            edge = wrapped(hi[k].astype(F32))
            ext[144:216, :] = jnp.where(me < BANDS - 1, edge, 0.0).astype(BF)

    loads[1].wait()
    loads[3].wait()
    c0 = math.sqrt(2.0 / math.pi)
    spec = jnp.zeros((2 * M, 384), F32)
    for k in range(2):
        ext[0:72, :] = wrapped(x[k, 0])
        ext[72:144, :] = wrapped(x[k, 1])
        for h in range(2):
            halos[k][h].wait_recv()
            fill_halo(low, high, k, h)
            v = x[k, h].astype(F32) + conv_half(weights, ext, prod, h)
            sq = v * v
            t = jnp.tanh(c0 * v * (1.0 + 0.044715 * sq))
            half = 0.5 * (1.0 + t)
            act[h * 72 : (h + 1) * 72, :] = (v * half).astype(BF)
            slope[k, h] = (half + 0.5 * v * (1.0 - t * t) * (c0 * (1.0 + 0.134145 * sq))).astype(BF)
        waves = lax.dot_general(
            table[...], act[...], (((1,), (1,)), ((), ())), preferred_element_type=F32
        ).astype(BF)
        spec = spec + jnp.dot(waves, placing[k], preferred_element_type=F32)
        if k == 0:
            legx.arrived()
            legx2 = Exchange(
                "ens", ENS, em, lambda p: legrecv, lambda m: legall.at[m],
                legall.at[pl.ds(0, ENS - 1)], legall.at[pl.ds(0, ENS - 1)], leg2_sems,
            )
            legx2.start()
            legall[em] = legrecv[...]
    spec = spec.astype(BF)
    lined = jnp.concatenate(
        [
            jnp.concatenate(
                [spec[a * 32 : (a + 1) * 32, t * 128 : (t + 1) * 128] for a in range(10)], axis=1
            )
            for t in range(3)
        ],
        axis=0,
    )
    loads[7].wait()
    lined = jnp.dot(lined, regroup[...], preferred_element_type=F32)

    def tile(e, t):
        return pl.ds(e * 128 + t, BANDS, stride=4)

    for e in range(ENS):
        for t in range(3):
            flat[tile(e, t), :] = lined[t * 32 : (t + 1) * 32, e * 128 : (e + 1) * 128]
        flat[tile(e, 3), :] = jnp.zeros((BANDS, 128), F32)
    send1[...] = flat[...].reshape(WORLD, 4, 128).astype(BF)
    self_at = em * BANDS + me

    pl.semaphore_wait(entered, ENS - 1)
    x1 = Everyone(send1, recv1, em, me, sems1)
    x1.start()
    recv1[self_at] = send1[self_at]

    loads[2].wait()
    wide[0] = window[:, :, :, 0:128].astype(F32).reshape(2 * C, 16, 128)
    wide[1] = jnp.concatenate(
        [
            window[:, :, :, 128:L].astype(F32).reshape(2 * C, 16, L - 128),
            jnp.zeros((2 * C, 16, 256 - L), F32),
        ],
        axis=2,
    )
    lane = iota((80, 128), 1)

    def folded(v):
        return jnp.where(
            lane % 64 < 60, jnp.where(lane < 64, v[0:80], pltpu.roll(v[80:160], 64, 1)), 0.0
        )

    cr, at = iota((2 * C, 128), 0), iota((2 * C, 128), 1)
    mine = (cr // 2 == em * SHARE + at % 3) & (cr % 2 == at % 12 // 6)
    goal0, goal1 = jnp.zeros((128, 128), F32), jnp.zeros((128, 128), F32)
    for ml in range(ORDERS):
        spot = onehot(mine & (at // 12 == ml))
        for b in range(2):
            part = wide[b, :, m0 - base + ml, :].astype(BF)
            t = lax.dot_general(part, spot, (((0,), (0,)), ((), ())), preferred_element_type=F32)
            if b == 0:
                goal0 = goal0 + t
            else:
                goal1 = goal1 + t
    target[...] = folded(jnp.concatenate([goal0, goal1[0 : L - 128]], axis=0))
    place = iota((L, L), 0)
    spots = onehot(iota((L, L), 1) == place % BANDS * 5 + place // BANDS)
    loads[6].wait()
    kept = onehot(place == jnp.broadcast_to(order[...], (L, L)))
    chosen[...] = lax.dot_general(
        spots, kept, (((1,), (1,)), ((), ())), preferred_element_type=F32
    ).astype(BF)

    legx2.arrived()
    more[...] = legall[...].astype(F32)
    for ml in range(ORDERS):
        for i in range(ROWS):
            n, j = i * ORDERS + ml, (i % 2) * 3 + i // 2
            at = slice(j * 32, (j + 1) * 32)
            leg[ml, at, 0:128] = more[n // 4, :, n % 4 * 2, :].astype(BF)
            leg[ml, at, 128:L] = more[n // 4, :, n % 4 * 2 + 1, 0 : L - 128].astype(BF)
    mix_lanes(mix, mixing)

    x1.arrived()

    def arranged(recv):
        flat[...] = recv[...].astype(F32).reshape(WORLD * 4, 128)
        return jnp.concatenate(
            [
                jnp.concatenate([flat[tile(e, t), :] for e in range(ENS)], axis=1)
                for t in range(3)
            ],
            axis=0,
        )

    waves = arranged(recv1)
    kind = iota((96, 1024), 1) % 128 // 12
    acc = jnp.zeros((L, 1024), F32)
    for ml in range(ORDERS):
        both = jnp.concatenate(
            [jnp.where(kind == ml, waves, 0.0), jnp.where(kind == ml + 5, waves, 0.0)], axis=0
        ).astype(BF)
        acc = acc + lax.dot_general(
            leg[ml], both, (((0,), (0,)), ((), ())), preferred_element_type=F32
        )
    for e in range(ENS):
        v = acc[:, e * 128 : (e + 1) * 128]
        coeff[e] = folded(v + pltpu.roll(v, 68, 1))

    small = iota((16, 128), 1) % 64

    def other(v):
        return jnp.where(small % 6 < 3, pltpu.roll(v, 125, 1), pltpu.roll(v, 3, 1))

    def step(s, carry):
        at = pl.ds(pl.multiple_of(s * 16, 16), 16)
        u = [coeff[a, at, :] for a in range(ENS)]
        w = [jnp.where(small < 60, other(v), 0.0) for v in u]
        goal = target[at, :]
        plus = [jnp.zeros((16, 128), F32)] * ENS
        for b in range(ENS):
            turned = jnp.zeros((16, 128), F32)
            for a in range(b):
                one = soft_sign(u[a] - u[b])
                two = soft_sign(u[a] - w[b])
                plus[a] = plus[a] + (one + two)
                plus[b] = plus[b] - one
                turned = turned + two
            plus[b] = plus[b] + soft_sign(u[b] - w[b])
            plus[b] = plus[b] - jnp.where(small < 60, other(turned), 0.0)
        for a in range(ENS):
            coeff[a, at, :] = soft_sign(u[a] - goal) / 16.0 - plus[a] / 240.0
        return carry

    lax.fori_loop(0, 5, step, 0)
    for e in range(ENS):
        g = coeff[e]
        tall = jnp.concatenate([g, pltpu.roll(g, 64, 1)], axis=0)
        grads[:, e * 128 : (e + 1) * 128] = jnp.where(iota((L, 128), 1) < 60, tall, 0.0).astype(BF)
    kind = iota((L, 1024), 1) % 128 // 12
    acc = jnp.zeros((192, 1024), F32)
    for ml in range(ORDERS):
        g = jnp.where(kind == ml, grads[...].astype(F32), 0.0).astype(BF)
        acc = acc + jnp.dot(leg[ml], g, preferred_element_type=F32)
    for e in range(ENS):
        for t in range(3):
            even = acc[t * 32 : (t + 1) * 32, e * 128 : (e + 1) * 128]
            odd = acc[96 + t * 32 : 96 + (t + 1) * 32, e * 128 : (e + 1) * 128]
            flat[tile(e, t), :] = even + pltpu.roll(odd, 60, 1)
    send4[...] = flat[...].reshape(WORLD, 4, 128).astype(BF)
    x4 = Everyone(send4, recv4, em, me, sems4)
    x4.start()
    recv4[self_at] = send4[self_at]
    o = jnp.dot(chosen[...], grads[...], preferred_element_type=F32)
    for e in range(ENS):
        part = [o[j * 32 : (j + 1) * 32, e * 128 : (e + 1) * 128] for j in range(5)]
        for t in range(2):
            flat[tile(e, t), :] = part[2 * t] + pltpu.roll(part[2 * t + 1], 64, 1)
        flat[tile(e, 2), :] = part[4]
    send5[...] = flat[...].reshape(WORLD, 4, 128).astype(BF)
    x5 = Everyone(send5, recv5, em, me, sems5)
    recv5[self_at] = send5[self_at]

    spread_weights(taps, flipped, wtmp, True)
    x4.arrived()
    x5.start()
    lined = jnp.dot(arranged(recv4).astype(BF), mixing[...], preferred_element_type=F32)
    for t in range(3):
        for r in range(2):
            q = jnp.concatenate(
                [
                    lined[t * 32 : (t + 1) * 32, (r * 5 + ml) * 128 : (r * 5 + ml + 1) * 128]
                    for ml in range(ORDERS)
                ],
                axis=0,
            )
            qt = q.T
            for par in range(2):
                for k in range(2):
                    at = par * 64 + k * C
                    i = 2 * t + par
                    left[r, k, i * C : (i + 1) * C, :] = qt[at : at + C, :]
    halos2 = []
    for k in range(2):
        grad = jnp.dot(left[0, k].astype(BF), table[0:M, :], preferred_element_type=F32)
        grad = grad + jnp.dot(left[1, k].astype(BF), table[M:, :], preferred_element_type=F32)
        for h in range(2):
            hid[k, h] = (grad[h * 72 : (h + 1) * 72] * slope[k, h].astype(F32)).astype(BF)
        pair = halo(hid, low2, high2, halo2_sems, k)
        for copy in pair:
            copy.start()
        halos2.append(pair)

    for k in range(2):
        ext[0:72, :] = wrapped(hid[k, 0])
        ext[72:144, :] = wrapped(hid[k, 1])
        for h in range(2):
            halos2[k][h].wait_recv()
            fill_halo(low2, high2, k, h)
            out[k, h] = (hid[k, h].astype(F32) + conv_half(flipped, ext, prod, h)).astype(BF)
        if k == 0:
            x5.arrived()
            got = arranged(recv5)
            lined = []
            for j in range(5):
                v = got[j // 2 * 32 : j // 2 * 32 + 32]
                if j % 2:
                    v = jnp.concatenate(
                        [pltpu.roll(v[:, e * 128 : (e + 1) * 128], 64, 1) for e in range(ENS)], axis=1
                    )
                lined.append(v)
            lined = jnp.concatenate(lined, axis=0).astype(BF)
            loads[8].wait()
            lined = jnp.dot(lined, regroup5[...], preferred_element_type=F32)
            for j in range(5):
                for ml in range(ORDERS):
                    turn[pl.ds(ml, BANDS, stride=ORDERS), :] = lined[
                        j * 32 : (j + 1) * 32, ml * 128 : (ml + 1) * 128
                    ]
                qt = turn[...].T
                for r in range(2):
                    for k in range(2):
                        score[k, :, j, r, :] = qt[r * 64 + k * 24 : r * 64 + k * 24 + 24, :]

    for pairs in (halos, halos2):
        for pair in pairs:
            for copy in pair:
                copy.wait_send()
    for exchange in (legx, legx2, x1, x4, x5):
        exchange.done()


HALF = (2, 2, 72, NLON)
CHUNK = (WORLD, 4, 128)


def whole(*args):
    vmem = pl.BlockSpec(memory_space=pltpu.VMEM)
    far = pl.BlockSpec(memory_space=pltpu.HBM)
    pair = pltpu.SemaphoreType.DMA((2,))
    halo = (2, 72, NLON)
    eighth = (BANDS, 8, 128)
    scratch = [
        (HALF, BF), ((ROWS, M, L), BF), ((2 * M, NLON), BF), ((7, 7, C), F32), ((C, C), BF),
        ((1, L), jnp.int32), ((C, 2, 16, L), BF),
        ((2, 2 * C, 16, 128), F32), ((7, 7, 216), F32), ((2, 144, 384), BF), ((80, 128), F32),
        ((L, L), BF),
        (halo, BF), (halo, BF), (halo, BF), (halo, BF),
        ((2, 504, 216), BF), ((2, 504, 216), BF), ((504, 216), F32),
        ((216, 1536), BF), ((504, 1536), F32), ((144, NLON), BF), (HALF, BF), (HALF, BF),
        ((2, ROWS, M, 128), F32), (eighth, BF), (eighth, BF), ((ENS,) + eighth, BF),
        ((ORDERS, 192, L), BF),
        ((WORLD * 4, 128), F32), (eighth, F32), ((ENS,) + eighth, F32), (CHUNK, BF), (CHUNK, BF),
        ((ENS, 80, 128), F32), ((L, 1024), BF), (CHUNK, BF), (CHUNK, BF), (CHUNK, BF), (CHUNK, BF),
        ((2, 2, 144, M), F32), ((M, 128), F32),
        ((1280, 1024), BF), ((1024, 1280), BF), ((1024, 640), BF),
    ]
    return pl.pallas_call(
        kernel,
        out_shape=[
            jax.ShapeDtypeStruct(HALF, BF),
            jax.ShapeDtypeStruct((2, C, 5, 2, M), F32),
        ],
        in_specs=[far] * len(args),
        out_specs=[vmem, vmem],
        scratch_shapes=[pltpu.VMEM(s, d) for s, d in scratch]
        + [pltpu.SemaphoreType.DMA((9,))]
        + [pltpu.SemaphoreType.DMA((4, 2))] * 2
        + [pair] * 5
        + [pltpu.SemaphoreType.REGULAR],
        compiler_params=pltpu.CompilerParams(
            vmem_limit_bytes=62 << 20, collective_id=0, has_side_effects=True
        ),
    )(*args)


def local(fields, depth_kernel, mix_weight, legendre, truth, degree_order):
    table = jnp.asarray(wave_table())
    x = jnp.transpose(fields, (0, 2, 1, 3)).reshape(HALF)
    kern = jnp.transpose(depth_kernel, (1, 2, 0))
    out, score = whole(
        x, legendre, kern, table, mix_weight, truth, degree_order.reshape(1, L),
        jnp.asarray(gather_lanes()), jnp.asarray(scatter_lanes()),
    )
    grad_fields = jnp.transpose(out.reshape(2, ROWS, C, NLON), (0, 2, 1, 3))
    return grad_fields, jnp.transpose(score, (0, 1, 3, 4, 2))


def solution(mesh):
    placed = (P("ens", None, "lat", None), P(), P(), P("lat", None, None), P(), P())
    return jax.shard_map(
        local,
        mesh=mesh,
        in_specs=placed,
        out_specs=(P("ens", None, "lat", None), P("ens", None, None, None, "lat")),
        check_vma=False,
    )
```
